32 devices in a mesh: ctx: 8 (over z, y), mp: 4 (over x, core).
Axes of the slice: x: 2, y: 2, z: 4, core: 2. Of those that a mesh axis runs over, the one named last changes fastest.
Arguments:
- tokens: bfloat16 [3072, 6144], P('ctx', 'mp'), may hold values from -24 to 24, as said below
- qkv_weight: bfloat16 [6144, 3, 24, 128], P('ctx', None, 'mp'), may hold values from -1 to 1, as said below
Outputs:
- attended: bfloat16 [3072, 24, 128], P('ctx', 'mp')
The draws below stay inside these ranges and needn't reach their ends.
Inputs may be any that keep to these rules, and one draw needn't show every extreme that they name: `tokens`: finite values. `qkv_weight`: entries lie within 8 / sqrt(6144) of zero.
All inputs are finite; a program needn't handle non-finite values.
Results may differ from the reference program's by a relative error of at most 0.0045.
The reference program's roundings to bfloat16 on the way (of `projected` and `probs`) count: a program that leaves them out, or rounds other values in their place, can miss the bound.
Values may be sent and summed in bfloat16 or wider, within the bound.
No kernel may reach another device: no remote copies, remote signals or barrier semaphores. Data moves between devices by JAX's collectives and lax.ppermute only.
A program may use at most 128 MiB of HBM per device.

```python
import math
import jax
import jax.numpy as jnp
from jax import lax

D = 6144
H = 24
HD = 128
REACH = 4
TOK_DEV = 384
TOKENS = 3072
N_CTX = 8


def draw_tokens(key, part):
    base = jax.random.normal(jax.random.fold_in(key, 11), (TOKENS // 2, 2, D), jnp.float32)
    values = jnp.clip(base, -6.0, 6.0)
    return values.reshape(TOKENS, D).astype(jnp.bfloat16)


def draw_qkv_weight(key, part):
    base = jax.random.normal(jax.random.fold_in(key, 21), (D, 3, H, HD), jnp.float32)
    factor = jnp.array([1.7, 1.7, 1.0], jnp.float32).reshape(1, 3, 1, 1)
    weight = base * factor / math.sqrt(D)
    bound = 8.0 / math.sqrt(D)
    return jnp.clip(weight, -bound, bound).astype(jnp.bfloat16)


def setup_inputs(seed: int = 0) -> dict:
    streams_of = jax.random.split(jax.random.key(seed), 3)
    return {
        "tokens": draw_tokens(jax.random.fold_in(streams_of[2], 71), 0),
        "qkv_weight": draw_qkv_weight(jax.random.fold_in(streams_of[2], 71), 0),
    }


def reference(tokens, qkv_weight):
    flat_weight = qkv_weight.reshape(D, 3 * H * HD)
    projected = jnp.dot(tokens, flat_weight, preferred_element_type=jnp.float32).astype(jnp.bfloat16)
    projected = projected.reshape(TOKENS, 3, H, HD)
    queries = projected[:, 0]
    key_all = projected[:, 1]
    value_all = projected[:, 2]
    scale = 1.0 / (HD ** 0.5)

    def one_block(block):
        start = (block * TOK_DEV).astype(jnp.int32)
        query_rows = lax.dynamic_slice_in_dim(queries, start, TOK_DEV, 0)
        key_parts = []
        value_parts = []
        for offset in range(REACH):
            other = (((block - offset) % N_CTX) * TOK_DEV).astype(jnp.int32)
            key_parts.append(lax.dynamic_slice_in_dim(key_all, other, TOK_DEV, 0))
            value_parts.append(lax.dynamic_slice_in_dim(value_all, other, TOK_DEV, 0))
        key_rows = jnp.concatenate(key_parts, axis=0).astype(jnp.float32)
        value_rows = jnp.concatenate(value_parts, axis=0).astype(jnp.float32)
        scores = jnp.einsum("thd,shd->hts", query_rows.astype(jnp.float32), key_rows) * scale
        top = jnp.max(scores, axis=-1, keepdims=True)
        expo = jnp.exp(scores - top)
        totals = jnp.sum(expo, axis=-1, keepdims=True)
        probs = lax.optimization_barrier(expo.astype(jnp.bfloat16))
        mixed = jnp.einsum("hts,shd->htd", probs.astype(jnp.float32), value_rows) / totals
        return jnp.transpose(mixed, (1, 0, 2)).astype(jnp.bfloat16)

    blocks = lax.map(one_block, jnp.arange(N_CTX, dtype=jnp.int32))
    return blocks.reshape(TOKENS, H, HD)
```

```python
import math

import jax
import jax.numpy as jnp
from jax import lax
from jax.sharding import PartitionSpec as P

REACH = 4


def ring_order(mesh):
    n = mesh.shape["ctx"]
    order = list(range(n))
    try:
        axis = mesh.axis_names.index("ctx")
        devices = mesh.devices.transpose([axis] + [a for a in range(mesh.devices.ndim) if a != axis])
        devices = devices.reshape(n, -1)[:, 0]
        coords = [tuple(d.coords) for d in devices]
    except Exception:
        return order
    if len(set(coords)) != n:
        return order

    def near(a, b):
        return sum(abs(i - j) for i, j in zip(coords[a], coords[b])) == 1

    neighbours = [[b for b in range(n) if b != a and near(a, b)] for a in range(n)]
    path, seen, budget = [0], {0}, [20000]

    def search():
        budget[0] -= 1
        if budget[0] < 0:
            return False
        if len(path) == n:
            return near(path[-1], path[0]) or n <= 2
        for b in sorted(neighbours[path[-1]], key=lambda b: len([x for x in neighbours[b] if x not in seen])):
            if b in seen:
                continue
            path.append(b)
            seen.add(b)
            if search():
                return True
            path.pop()
            seen.discard(b)
        return False

    if search():
        return path
    return order


def shifted(array, axis, by):
    devices = lax.axis_size(axis)
    return lax.ppermute(array, axis, [(i, (i + by) % devices) for i in range(devices)])


def make_on_device(ring):
    n = len(ring)
    pos = [0] * n
    for i, c in enumerate(ring):
        pos[c] = i
    clockwise = [(ring[i], ring[(i + 1) % n]) for i in range(n)]
    counter = [(ring[i], ring[(i - 1) % n]) for i in range(n)]
    ring_arr = jnp.array(ring, jnp.int32)
    pos_arr = jnp.array(pos, jnp.int32)

    def on_device(tokens, qkv_weight):
        features = lax.all_gather(tokens, "mp", axis=1, tiled=True)
        rows_dev = features.shape[0]
        rows_w = qkv_weight.shape[0]
        heads_local = qkv_weight.shape[2]
        head_size = qkv_weight.shape[3]
        scale = 1.0 / math.sqrt(head_size)
        me = lax.axis_index("ctx")
        my_pos = pos_arr[me]

        def partial(block, piece, offset):
            start = block * rows_w + offset
            cols = lax.dynamic_slice_in_dim(features, start, piece.shape[0], axis=1)
            flat = piece.reshape(piece.shape[0], -1)
            return jnp.dot(cols, flat, preferred_element_type=jnp.float32)

        total = partial(me, qkv_weight, 0)
        going_cw = qkv_weight
        going_ccw = qkv_weight
        full_steps = (n - 1) // 2
        for step in range(1, full_steps + 1):
            going_cw = lax.ppermute(going_cw, "ctx", clockwise)
            going_ccw = lax.ppermute(going_ccw, "ctx", counter)
            total = total + partial(ring_arr[(my_pos - step) % n], going_cw, 0)
            total = total + partial(ring_arr[(my_pos + step) % n], going_ccw, 0)
        if n % 2 == 0 and n > 1:
            step = n // 2
            far = ring_arr[(my_pos + step) % n]
            if rows_w % 2 == 0:
                half = rows_w // 2
                last_cw = lax.ppermute(going_cw[:half], "ctx", clockwise)
                last_ccw = lax.ppermute(going_ccw[half:], "ctx", counter)
                total = total + partial(far, last_cw, 0)
                total = total + partial(far, last_ccw, half)
            else:
                last_cw = lax.ppermute(going_cw, "ctx", clockwise)
                total = total + partial(far, last_cw, 0)

        projected = total.astype(jnp.bfloat16).reshape(rows_dev, 3, heads_local, head_size)
        queries = projected[:, 0]
        key_value = projected[:, 1:]
        blocks = [key_value] + [shifted(key_value, "ctx", by) for by in range(1, REACH)]
        key_rows = jnp.concatenate([block[:, 0] for block in blocks], axis=0)
        value_rows = jnp.concatenate([block[:, 1] for block in blocks], axis=0)
        scores = (
            jnp.einsum("thd,shd->hts", queries, key_rows, preferred_element_type=jnp.float32) * scale
        )
        top = jnp.max(scores, axis=-1, keepdims=True)
        expo = jnp.exp(scores - top)
        totals = jnp.sum(expo, axis=-1, keepdims=True)
        probs = expo.astype(jnp.bfloat16)
        mixed = (
            jnp.einsum("hts,shd->htd", probs, value_rows, preferred_element_type=jnp.float32) / totals
        )
        return jnp.transpose(mixed, (1, 0, 2)).astype(jnp.bfloat16)

    return on_device


def solution(mesh):
    placed = (P("ctx", "mp"), P("ctx", None, "mp", None))
    return jax.shard_map(
        make_on_device(ring_order(mesh)),
        mesh=mesh,
        in_specs=placed,
        out_specs=P("ctx", "mp", None),
        check_vma=False,
    )
```

```python
import math

import jax
import jax.numpy as jnp
from jax import lax
from jax.sharding import PartitionSpec as P

REACH = 4


def ring_order(mesh):
    n = mesh.shape["ctx"]
    order = list(range(n))
    try:
        axis = mesh.axis_names.index("ctx")
        devices = mesh.devices.transpose([axis] + [a for a in range(mesh.devices.ndim) if a != axis])
        devices = devices.reshape(n, -1)[:, 0]
        coords = [tuple(d.coords) for d in devices]
    except Exception:
        return order
    if len(set(coords)) != n:
        return order

    def near(a, b):
        return sum(abs(i - j) for i, j in zip(coords[a], coords[b])) == 1

    neighbours = [[b for b in range(n) if b != a and near(a, b)] for a in range(n)]
    path, seen, budget = [0], {0}, [20000]

    def search():
        budget[0] -= 1
        if budget[0] < 0:
            return False
        if len(path) == n:
            return near(path[-1], path[0]) or n <= 2
        for b in sorted(neighbours[path[-1]], key=lambda b: len([x for x in neighbours[b] if x not in seen])):
            if b in seen:
                continue
            path.append(b)
            seen.add(b)
            if search():
                return True
            path.pop()
            seen.discard(b)
        return False

    if search():
        return path
    return order


def shifted(array, axis, by):
    devices = lax.axis_size(axis)
    return lax.ppermute(array, axis, [(i, (i + by) % devices) for i in range(devices)])


def make_on_device(ring):
    n = len(ring)
    pos = [0] * n
    for i, c in enumerate(ring):
        pos[c] = i
    clockwise = [(ring[i], ring[(i + 1) % n]) for i in range(n)]
    counter = [(ring[i], ring[(i - 1) % n]) for i in range(n)]
    ring_arr = jnp.array(ring, jnp.int32)
    pos_arr = jnp.array(pos, jnp.int32)

    def ring_project(features, piece, me):
        rows_w = piece.shape[0]
        my_pos = pos_arr[me]

        def partial(block, part, offset):
            start = block * rows_w + offset
            cols = lax.dynamic_slice_in_dim(features, start, part.shape[0], axis=1)
            flat = part.reshape(part.shape[0], -1)
            return jnp.dot(cols, flat, preferred_element_type=jnp.float32)

        total = partial(me, piece, 0)
        going_cw = piece
        going_ccw = piece
        for step in range(1, (n - 1) // 2 + 1):
            going_cw = lax.ppermute(going_cw, "ctx", clockwise)
            going_ccw = lax.ppermute(going_ccw, "ctx", counter)
            total = total + partial(ring_arr[(my_pos - step) % n], going_cw, 0)
            total = total + partial(ring_arr[(my_pos + step) % n], going_ccw, 0)
        if n % 2 == 0 and n > 1:
            far = ring_arr[(my_pos + n // 2) % n]
            if rows_w % 2 == 0:
                half = rows_w // 2
                last_cw = lax.ppermute(going_cw[:half], "ctx", clockwise)
                last_ccw = lax.ppermute(going_ccw[half:], "ctx", counter)
                total = total + partial(far, last_cw, 0)
                total = total + partial(far, last_ccw, half)
            else:
                last_cw = lax.ppermute(going_cw, "ctx", clockwise)
                total = total + partial(far, last_cw, 0)
        return total

    def earlier_blocks(key_value, me):
        if n % 2 or n < 4 or REACH != 4:
            return [shifted(key_value, "ctx", by) for by in range(1, REACH)]
        two_back = shifted(key_value, "ctx", 2)
        to_odd = lax.ppermute(
            jnp.stack([key_value, two_back]), "ctx", [(e, e + 1) for e in range(0, n, 2)]
        )
        to_even = lax.ppermute(two_back, "ctx", [(o, o - 1) for o in range(1, n, 2)])
        three_back = lax.ppermute(to_even, "ctx", [(e, (e + 2) % n) for e in range(0, n, 2)])
        odd = (me % 2) == 1
        one_back = jnp.where(odd, to_odd[0], to_even)
        three_back = jnp.where(odd, to_odd[1], three_back)
        return [one_back, two_back, three_back]

    def on_device(tokens, qkv_weight):
        features = lax.all_gather(tokens, "mp", axis=1, tiled=True)
        rows_dev = features.shape[0]
        heads_local = qkv_weight.shape[2]
        head_size = qkv_weight.shape[3]
        scale = 1.0 / math.sqrt(head_size)
        me = lax.axis_index("ctx")

        kv_total = ring_project(features, qkv_weight[:, 1:], me)
        key_value = kv_total.astype(jnp.bfloat16).reshape(rows_dev, 2, heads_local, head_size)
        q_piece, key_value = lax.optimization_barrier((qkv_weight[:, 0], key_value))
        blocks = [key_value] + earlier_blocks(key_value, me)
        q_total = ring_project(features, q_piece, me)
        queries = q_total.astype(jnp.bfloat16).reshape(rows_dev, heads_local, head_size)

        key_rows = jnp.concatenate([block[:, 0] for block in blocks], axis=0)
        value_rows = jnp.concatenate([block[:, 1] for block in blocks], axis=0)
        scores = (
            jnp.einsum("thd,shd->hts", queries, key_rows, preferred_element_type=jnp.float32) * scale
        )
        top = jnp.max(scores, axis=-1, keepdims=True)
        expo = jnp.exp(scores - top)
        totals = jnp.sum(expo, axis=-1, keepdims=True)
        probs = expo.astype(jnp.bfloat16)
        mixed = (
            jnp.einsum("hts,shd->htd", probs, value_rows, preferred_element_type=jnp.float32) / totals
        )
        return jnp.transpose(mixed, (1, 0, 2)).astype(jnp.bfloat16)

    return on_device


def solution(mesh):
    placed = (P("ctx", "mp"), P("ctx", None, "mp", None))
    return jax.shard_map(
        make_on_device(ring_order(mesh)),
        mesh=mesh,
        in_specs=placed,
        out_specs=P("ctx", "mp", None),
        check_vma=False,
    )
```

```python
import functools
import math

import jax
import jax.numpy as jnp
from jax import lax
from jax.experimental import pallas as pl
from jax.experimental.pallas import tpu as pltpu
from jax.sharding import PartitionSpec as P

REACH = 4


def attention_kernel(scale, reach, q_ref, *refs):
    k_refs = refs[:reach]
    v_refs = refs[reach : 2 * reach]
    o_ref = refs[2 * reach]
    q = q_ref[...]
    scores = [
        lax.dot_general(q, k_ref[...], (((1,), (1,)), ((), ())), preferred_element_type=jnp.float32) * scale
        for k_ref in k_refs
    ]
    top = scores[0].max(axis=-1, keepdims=True)
    for s in scores[1:]:
        top = jnp.maximum(top, s.max(axis=-1, keepdims=True))
    expos = [jnp.exp(s - top) for s in scores]
    totals = expos[0].sum(axis=-1, keepdims=True)
    for e in expos[1:]:
        totals = totals + e.sum(axis=-1, keepdims=True)
    mixed = jnp.dot(expos[0].astype(jnp.bfloat16), v_refs[0][...], preferred_element_type=jnp.float32)
    for e, v_ref in zip(expos[1:], v_refs[1:]):
        mixed = mixed + jnp.dot(e.astype(jnp.bfloat16), v_ref[...], preferred_element_type=jnp.float32)
    o_ref[...] = (mixed / totals).astype(o_ref.dtype)


def windowed_attention(queries, blocks, scale):
    rows, heads, size = queries.shape
    reach = len(blocks)
    q2d = queries.reshape(rows, heads * size)
    kv2d = [block.reshape(rows, 2 * heads * size) for block in blocks]
    q_spec = pl.BlockSpec((rows, size), lambda h: (0, h))
    v_spec = pl.BlockSpec((rows, size), lambda h: (0, h + heads))
    keys = rows * reach
    cost = pl.CostEstimate(
        flops=4 * rows * keys * size * heads,
        transcendentals=rows * keys * heads,
        bytes_accessed=2 * (2 * rows * heads * size + 2 * keys * heads * size),
    )
    out = pl.pallas_call(
        functools.partial(attention_kernel, scale, reach),
        out_shape=jax.ShapeDtypeStruct((rows, heads * size), jnp.bfloat16),
        grid=(heads,),
        in_specs=[q_spec] + [q_spec] * reach + [v_spec] * reach,
        out_specs=q_spec,
        cost_estimate=cost,
    )(q2d, *kv2d, *kv2d)
    return out.reshape(rows, heads, size)


def ring_order(mesh):
    n = mesh.shape["ctx"]
    order = list(range(n))
    try:
        axis = mesh.axis_names.index("ctx")
        devices = mesh.devices.transpose([axis] + [a for a in range(mesh.devices.ndim) if a != axis])
        devices = devices.reshape(n, -1)[:, 0]
        coords = [tuple(d.coords) for d in devices]
    except Exception:
        return order
    if len(set(coords)) != n:
        return order

    def near(a, b):
        return sum(abs(i - j) for i, j in zip(coords[a], coords[b])) == 1

    neighbours = [[b for b in range(n) if b != a and near(a, b)] for a in range(n)]
    path, seen, budget = [0], {0}, [20000]

    def search():
        budget[0] -= 1
        if budget[0] < 0:
            return False
        if len(path) == n:
            return near(path[-1], path[0]) or n <= 2
        for b in sorted(neighbours[path[-1]], key=lambda b: len([x for x in neighbours[b] if x not in seen])):
            if b in seen:
                continue
            path.append(b)
            seen.add(b)
            if search():
                return True
            path.pop()
            seen.discard(b)
        return False

    if search():
        return path
    return order


def shifted(array, axis, by):
    devices = lax.axis_size(axis)
    return lax.ppermute(array, axis, [(i, (i + by) % devices) for i in range(devices)])


def make_on_device(ring):
    n = len(ring)
    pos = [0] * n
    for i, c in enumerate(ring):
        pos[c] = i
    clockwise = [(ring[i], ring[(i + 1) % n]) for i in range(n)]
    counter = [(ring[i], ring[(i - 1) % n]) for i in range(n)]
    ring_arr = jnp.array(ring, jnp.int32)
    pos_arr = jnp.array(pos, jnp.int32)

    def ring_project(features, piece, me):
        rows_w = piece.shape[0]
        my_pos = pos_arr[me]

        def partial(block, part, offset):
            start = block * rows_w + offset
            cols = lax.dynamic_slice_in_dim(features, start, part.shape[0], axis=1)
            flat = part.reshape(part.shape[0], -1)
            return jnp.dot(cols, flat, preferred_element_type=jnp.float32)

        total = partial(me, piece, 0)
        going_cw = piece
        going_ccw = piece
        for step in range(1, (n - 1) // 2 + 1):
            going_cw = lax.ppermute(going_cw, "ctx", clockwise)
            going_ccw = lax.ppermute(going_ccw, "ctx", counter)
            total = total + partial(ring_arr[(my_pos - step) % n], going_cw, 0)
            total = total + partial(ring_arr[(my_pos + step) % n], going_ccw, 0)
        if n % 2 == 0 and n > 1:
            far = ring_arr[(my_pos + n // 2) % n]
            if rows_w % 2 == 0:
                half = rows_w // 2
                last_cw = lax.ppermute(going_cw[:half], "ctx", clockwise)
                last_ccw = lax.ppermute(going_ccw[half:], "ctx", counter)
                total = total + partial(far, last_cw, 0)
                total = total + partial(far, last_ccw, half)
            else:
                last_cw = lax.ppermute(going_cw, "ctx", clockwise)
                total = total + partial(far, last_cw, 0)
        return total

    def earlier_blocks(key_value, me):
        if n % 2 or n < 4 or REACH != 4:
            return [shifted(key_value, "ctx", by) for by in range(1, REACH)]
        two_back = shifted(key_value, "ctx", 2)
        to_odd = lax.ppermute(
            jnp.stack([key_value, two_back]), "ctx", [(e, e + 1) for e in range(0, n, 2)]
        )
        to_even = lax.ppermute(two_back, "ctx", [(o, o - 1) for o in range(1, n, 2)])
        three_back = lax.ppermute(to_even, "ctx", [(e, (e + 2) % n) for e in range(0, n, 2)])
        odd = (me % 2) == 1
        one_back = jnp.where(odd, to_odd[0], to_even)
        three_back = jnp.where(odd, to_odd[1], three_back)
        return [one_back, two_back, three_back]

    def on_device(tokens, qkv_weight):
        features = lax.all_gather(tokens, "mp", axis=1, tiled=True)
        rows_dev = features.shape[0]
        heads_local = qkv_weight.shape[2]
        head_size = qkv_weight.shape[3]
        scale = 1.0 / math.sqrt(head_size)
        me = lax.axis_index("ctx")

        kv_total = ring_project(features, qkv_weight[:, 1:], me)
        key_value = kv_total.astype(jnp.bfloat16).reshape(rows_dev, 2, heads_local, head_size)
        q_piece, key_value = lax.optimization_barrier((qkv_weight[:, 0], key_value))
        blocks = [key_value] + earlier_blocks(key_value, me)
        q_total = ring_project(features, q_piece, me)
        queries = q_total.astype(jnp.bfloat16).reshape(rows_dev, heads_local, head_size)

        return windowed_attention(queries, blocks, scale)

    return on_device


def solution(mesh):
    placed = (P("ctx", "mp"), P("ctx", None, "mp", None))
    return jax.shard_map(
        make_on_device(ring_order(mesh)),
        mesh=mesh,
        in_specs=placed,
        out_specs=P("ctx", "mp", None),
        check_vma=False,
    )
```

```python
import functools
import math

import jax
import jax.numpy as jnp
from jax import lax
from jax.experimental import pallas as pl
from jax.experimental.pallas import tpu as pltpu
from jax.sharding import PartitionSpec as P

REACH = 4


def attention_kernel(scale, reach, q_ref, *refs):
    k_refs = refs[:reach]
    v_refs = refs[reach : 2 * reach]
    o_ref = refs[2 * reach]
    q = q_ref[...]
    scores = [
        lax.dot_general(q, k_ref[...], (((1,), (1,)), ((), ())), preferred_element_type=jnp.float32) * scale
        for k_ref in k_refs
    ]
    top = scores[0].max(axis=-1, keepdims=True)
    for s in scores[1:]:
        top = jnp.maximum(top, s.max(axis=-1, keepdims=True))
    expos = [jnp.exp(s - top) for s in scores]
    totals = expos[0].sum(axis=-1, keepdims=True)
    for e in expos[1:]:
        totals = totals + e.sum(axis=-1, keepdims=True)
    mixed = jnp.dot(expos[0].astype(jnp.bfloat16), v_refs[0][...], preferred_element_type=jnp.float32)
    for e, v_ref in zip(expos[1:], v_refs[1:]):
        mixed = mixed + jnp.dot(e.astype(jnp.bfloat16), v_ref[...], preferred_element_type=jnp.float32)
    o_ref[...] = (mixed / totals).astype(o_ref.dtype)


def windowed_attention(queries, blocks, scale):
    rows, heads, size = queries.shape
    reach = len(blocks)
    q2d = queries.reshape(rows, heads * size)
    kv2d = [block.reshape(rows, 2 * heads * size) for block in blocks]
    q_spec = pl.BlockSpec((rows, size), lambda h: (0, h))
    v_spec = pl.BlockSpec((rows, size), lambda h: (0, h + heads))
    keys = rows * reach
    cost = pl.CostEstimate(
        flops=4 * rows * keys * size * heads,
        transcendentals=rows * keys * heads,
        bytes_accessed=2 * (2 * rows * heads * size + 2 * keys * heads * size),
    )
    out = pl.pallas_call(
        functools.partial(attention_kernel, scale, reach),
        out_shape=jax.ShapeDtypeStruct((rows, heads * size), jnp.bfloat16),
        grid=(heads,),
        in_specs=[q_spec] + [q_spec] * reach + [v_spec] * reach,
        out_specs=q_spec,
        cost_estimate=cost,
    )(q2d, *kv2d, *kv2d)
    return out.reshape(rows, heads, size)


def ctx_coords(mesh):
    n = mesh.shape["ctx"]
    axis = mesh.axis_names.index("ctx")
    devices = mesh.devices.transpose([axis] + [a for a in range(mesh.devices.ndim) if a != axis])
    return [tuple(d.coords) for d in devices.reshape(n, -1)[:, 0]]


def grid_layout(mesh):
    try:
        coords = ctx_coords(mesh)
    except Exception:
        return None
    n = len(coords)
    if n != 8 or len(set(coords)) != n:
        return None
    varying = [a for a in range(len(coords[0])) if len({c[a] for c in coords}) > 1]
    if len(varying) != 2:
        return None
    sizes = {a: sorted({c[a] for c in coords}) for a in varying}
    line = [a for a in varying if len(sizes[a]) == 4]
    pair = [a for a in varying if len(sizes[a]) == 2]
    if len(line) != 1 or len(pair) != 1:
        return None
    lin = [sizes[line[0]].index(c[line[0]]) for c in coords]
    pr = [sizes[pair[0]].index(c[pair[0]]) for c in coords]
    if sizes[line[0]] != list(range(sizes[line[0]][0], sizes[line[0]][0] + 4)):
        return None
    if sizes[pair[0]][1] - sizes[pair[0]][0] != 1:
        return None
    return lin, pr


def ring_order(mesh):
    n = mesh.shape["ctx"]
    order = list(range(n))
    try:
        axis = mesh.axis_names.index("ctx")
        devices = mesh.devices.transpose([axis] + [a for a in range(mesh.devices.ndim) if a != axis])
        devices = devices.reshape(n, -1)[:, 0]
        coords = [tuple(d.coords) for d in devices]
    except Exception:
        return order
    if len(set(coords)) != n:
        return order

    def near(a, b):
        return sum(abs(i - j) for i, j in zip(coords[a], coords[b])) == 1

    neighbours = [[b for b in range(n) if b != a and near(a, b)] for a in range(n)]
    path, seen, budget = [0], {0}, [20000]

    def search():
        budget[0] -= 1
        if budget[0] < 0:
            return False
        if len(path) == n:
            return near(path[-1], path[0]) or n <= 2
        for b in sorted(neighbours[path[-1]], key=lambda b: len([x for x in neighbours[b] if x not in seen])):
            if b in seen:
                continue
            path.append(b)
            seen.add(b)
            if search():
                return True
            path.pop()
            seen.discard(b)
        return False

    if search():
        return path
    return order


def shifted(array, axis, by):
    devices = lax.axis_size(axis)
    return lax.ppermute(array, axis, [(i, (i + by) % devices) for i in range(devices)])


def make_on_device(ring, layout):
    n = len(ring)
    pos = [0] * n
    for i, c in enumerate(ring):
        pos[c] = i
    clockwise = [(ring[i], ring[(i + 1) % n]) for i in range(n)]
    counter = [(ring[i], ring[(i - 1) % n]) for i in range(n)]
    ring_arr = jnp.array(ring, jnp.int32)
    pos_arr = jnp.array(pos, jnp.int32)

    def ring_project(features, piece, me):
        rows_w = piece.shape[0]
        my_pos = pos_arr[me]

        def partial(block, part, offset):
            start = block * rows_w + offset
            cols = lax.dynamic_slice_in_dim(features, start, part.shape[0], axis=1)
            flat = part.reshape(part.shape[0], -1)
            return jnp.dot(cols, flat, preferred_element_type=jnp.float32)

        total = partial(me, piece, 0)
        going_cw = piece
        going_ccw = piece
        for step in range(1, (n - 1) // 2 + 1):
            going_cw = lax.ppermute(going_cw, "ctx", clockwise)
            going_ccw = lax.ppermute(going_ccw, "ctx", counter)
            total = total + partial(ring_arr[(my_pos - step) % n], going_cw, 0)
            total = total + partial(ring_arr[(my_pos + step) % n], going_ccw, 0)
        if n % 2 == 0 and n > 1:
            far = ring_arr[(my_pos + n // 2) % n]
            if rows_w % 2 == 0:
                half = rows_w // 2
                last_cw = lax.ppermute(going_cw[:half], "ctx", clockwise)
                last_ccw = lax.ppermute(going_ccw[half:], "ctx", counter)
                total = total + partial(far, last_cw, 0)
                total = total + partial(far, last_ccw, half)
            else:
                last_cw = lax.ppermute(going_cw, "ctx", clockwise)
                total = total + partial(far, last_cw, 0)
        return total


    def spoke_project(tokens, features, piece, me, layout):
        lin, pr = layout
        at = {(lin[c], pr[c]): c for c in range(n)}
        ends = [c for c in range(n) if lin[c] in (0, 3)]
        middles = [c for c in range(n) if lin[c] in (1, 2)]
        spoke = {e: at[(1 if lin[e] == 0 else 2, pr[e])] for e in ends}
        end_of = {m: e for e, m in spoke.items()}
        ynbr = {c: at[(lin[c], 1 - pr[c])] for c in range(n)}
        znbr = {m: at[(3 - lin[m], pr[m])] for m in middles}
        rows_w = piece.shape[0]

        def table(values):
            return jnp.array([values.get(c, c) for c in range(n)], jnp.int32)[me]

        def partial(feats, block, part):
            cols = lax.dynamic_slice_in_dim(feats, block * rows_w, rows_w, axis=1)
            return jnp.dot(cols, part.reshape(rows_w, -1), preferred_element_type=jnp.float32)

        end_y = lax.ppermute(piece, "ctx", [(e, ynbr[e]) for e in ends])
        from_end = lax.ppermute(piece, "ctx", [(e, spoke[e]) for e in ends])
        relayed = lax.ppermute(end_y, "ctx", [(e, spoke[e]) for e in ends])
        mid_y = lax.ppermute(piece, "ctx", [(m, ynbr[m]) for m in middles])
        mid_z = lax.ppermute(piece, "ctx", [(m, znbr[m]) for m in middles])
        far_pair = lax.ppermute(jnp.stack([from_end, relayed]), "ctx", [(m, znbr[m]) for m in middles])
        far_y = lax.ppermute(mid_z, "ctx", [(m, ynbr[m]) for m in middles])
        end_tokens = lax.ppermute(tokens, "ctx", [(e, spoke[e]) for e in ends])
        end_features = lax.all_gather(end_tokens, "mp", axis=1, tiled=True)

        e_of = table(end_of)
        shared = [
            (me, piece),
            (table(ynbr), mid_y),
            (table(znbr), mid_z),
            (table({m: end_of[znbr[m]] for m in middles}), far_pair[0]),
            (table({m: ynbr[end_of[znbr[m]]] for m in middles}), far_pair[1]),
            (table({m: znbr[ynbr[m]] for m in middles}), far_y),
        ]
        end_partial = partial(end_features, *shared[0])
        for block, part in shared[1:]:
            end_partial = end_partial + partial(end_features, block, part)
        mid_total = partial(features, e_of, from_end) + partial(features, table({m: ynbr[end_of[m]] for m in middles}), relayed)
        for block, part in shared:
            mid_total = mid_total + partial(features, block, part)
        returned = lax.ppermute(end_partial, "ctx", [(m, end_of[m]) for m in middles])
        end_total = partial(features, me, piece) + partial(features, table(ynbr), end_y) + returned
        is_end = jnp.array([c in ends for c in range(n)])[me]
        return jnp.where(is_end, end_total, mid_total)

    def earlier_blocks(key_value, me):
        if n % 2 or n < 4 or REACH != 4:
            return [shifted(key_value, "ctx", by) for by in range(1, REACH)]
        two_back = shifted(key_value, "ctx", 2)
        to_odd = lax.ppermute(
            jnp.stack([key_value, two_back]), "ctx", [(e, e + 1) for e in range(0, n, 2)]
        )
        to_even = lax.ppermute(two_back, "ctx", [(o, o - 1) for o in range(1, n, 2)])
        three_back = lax.ppermute(to_even, "ctx", [(e, (e + 2) % n) for e in range(0, n, 2)])
        odd = (me % 2) == 1
        one_back = jnp.where(odd, to_odd[0], to_even)
        three_back = jnp.where(odd, to_odd[1], three_back)
        return [one_back, two_back, three_back]

    def on_device(tokens, qkv_weight):
        features = lax.all_gather(tokens, "mp", axis=1, tiled=True)
        rows_dev = features.shape[0]
        heads_local = qkv_weight.shape[2]
        head_size = qkv_weight.shape[3]
        scale = 1.0 / math.sqrt(head_size)
        me = lax.axis_index("ctx")

        if layout is None:
            project = lambda piece: ring_project(features, piece, me)
        else:
            project = lambda piece: spoke_project(tokens, features, piece, me, layout)
        kv_total = project(qkv_weight[:, 1:])
        key_value = kv_total.astype(jnp.bfloat16).reshape(rows_dev, 2, heads_local, head_size)
        q_piece, key_value = lax.optimization_barrier((qkv_weight[:, 0], key_value))
        blocks = [key_value] + earlier_blocks(key_value, me)
        q_total = project(q_piece)
        queries = q_total.astype(jnp.bfloat16).reshape(rows_dev, heads_local, head_size)

        return windowed_attention(queries, blocks, scale)

    return on_device


def solution(mesh):
    placed = (P("ctx", "mp"), P("ctx", None, "mp", None))
    return jax.shard_map(
        make_on_device(ring_order(mesh), grid_layout(mesh)),
        mesh=mesh,
        in_specs=placed,
        out_specs=P("ctx", "mp", None),
        check_vma=False,
    )
```

```python
import functools
import math

import jax
import jax.numpy as jnp
from jax import lax
from jax.experimental import pallas as pl
from jax.experimental.pallas import tpu as pltpu
from jax.sharding import PartitionSpec as P

REACH = 4


def attention_kernel(scale, reach, q_ref, *refs):
    k_refs = refs[:reach]
    v_refs = refs[reach : 2 * reach]
    o_ref = refs[2 * reach]
    q = q_ref[...]
    scores = [
        lax.dot_general(q, k_ref[...], (((0,), (0,)), ((), ())), preferred_element_type=jnp.float32) * scale
        for k_ref in k_refs
    ]
    top = scores[0].max(axis=-1, keepdims=True)
    for s in scores[1:]:
        top = jnp.maximum(top, s.max(axis=-1, keepdims=True))
    expos = [jnp.exp(s - top) for s in scores]
    totals = expos[0].sum(axis=-1, keepdims=True)
    for e in expos[1:]:
        totals = totals + e.sum(axis=-1, keepdims=True)
    mixed = None
    for e, v_ref in zip(expos, v_refs):
        term = lax.dot_general(
            e.astype(jnp.bfloat16), v_ref[...], (((1,), (1,)), ((), ())), preferred_element_type=jnp.float32
        )
        mixed = term if mixed is None else mixed + term
    o_ref[0] = (mixed / totals).astype(o_ref.dtype)


def windowed_attention(queries, blocks, scale):
    rows, heads, size = queries.shape
    reach = len(blocks)
    q_t = queries.reshape(rows, heads * size).T
    kv_t = [block.reshape(rows, 2 * heads * size).T for block in blocks]
    q_spec = pl.BlockSpec((size, rows), lambda h: (h, 0))
    v_spec = pl.BlockSpec((size, rows), lambda h: (h + heads, 0))
    keys = rows * reach
    cost = pl.CostEstimate(
        flops=4 * rows * keys * size * heads,
        transcendentals=rows * keys * heads,
        bytes_accessed=2 * (2 * rows * heads * size + 2 * keys * heads * size),
    )
    out = pl.pallas_call(
        functools.partial(attention_kernel, scale, reach),
        out_shape=jax.ShapeDtypeStruct((heads, rows, size), jnp.bfloat16),
        grid=(heads,),
        in_specs=[q_spec] + [q_spec] * reach + [v_spec] * reach,
        out_specs=pl.BlockSpec((1, rows, size), lambda h: (h, 0, 0)),
        cost_estimate=cost,
    )(q_t, *kv_t, *kv_t)
    return jnp.transpose(out, (1, 0, 2))


def ring_order(mesh):
    n = mesh.shape["ctx"]
    order = list(range(n))
    try:
        axis = mesh.axis_names.index("ctx")
        devices = mesh.devices.transpose([axis] + [a for a in range(mesh.devices.ndim) if a != axis])
        devices = devices.reshape(n, -1)[:, 0]
        coords = [tuple(d.coords) for d in devices]
    except Exception:
        return order
    if len(set(coords)) != n:
        return order

    def near(a, b):
        return sum(abs(i - j) for i, j in zip(coords[a], coords[b])) == 1

    neighbours = [[b for b in range(n) if b != a and near(a, b)] for a in range(n)]
    path, seen, budget = [0], {0}, [20000]

    def search():
        budget[0] -= 1
        if budget[0] < 0:
            return False
        if len(path) == n:
            return near(path[-1], path[0]) or n <= 2
        for b in sorted(neighbours[path[-1]], key=lambda b: len([x for x in neighbours[b] if x not in seen])):
            if b in seen:
                continue
            path.append(b)
            seen.add(b)
            if search():
                return True
            path.pop()
            seen.discard(b)
        return False

    if search():
        return path
    return order


def shifted(array, axis, by):
    devices = lax.axis_size(axis)
    return lax.ppermute(array, axis, [(i, (i + by) % devices) for i in range(devices)])


def make_on_device(ring):
    n = len(ring)
    pos = [0] * n
    for i, c in enumerate(ring):
        pos[c] = i
    clockwise = [(ring[i], ring[(i + 1) % n]) for i in range(n)]
    counter = [(ring[i], ring[(i - 1) % n]) for i in range(n)]
    ring_arr = jnp.array(ring, jnp.int32)
    pos_arr = jnp.array(pos, jnp.int32)

    def ring_project(features, piece, me):
        rows_w = piece.shape[0]
        my_pos = pos_arr[me]

        def partial(block, part, offset):
            start = block * rows_w + offset
            cols = lax.dynamic_slice_in_dim(features, start, part.shape[0], axis=1)
            flat = part.reshape(part.shape[0], -1)
            return jnp.dot(cols, flat, preferred_element_type=jnp.float32)

        total = partial(me, piece, 0)
        going_cw = piece
        going_ccw = piece
        for step in range(1, (n - 1) // 2 + 1):
            going_cw = lax.ppermute(going_cw, "ctx", clockwise)
            going_ccw = lax.ppermute(going_ccw, "ctx", counter)
            total = total + partial(ring_arr[(my_pos - step) % n], going_cw, 0)
            total = total + partial(ring_arr[(my_pos + step) % n], going_ccw, 0)
        if n % 2 == 0 and n > 1:
            far = ring_arr[(my_pos + n // 2) % n]
            if rows_w % 2 == 0:
                half = rows_w // 2
                last_cw = lax.ppermute(going_cw[:half], "ctx", clockwise)
                last_ccw = lax.ppermute(going_ccw[half:], "ctx", counter)
                total = total + partial(far, last_cw, 0)
                total = total + partial(far, last_ccw, half)
            else:
                last_cw = lax.ppermute(going_cw, "ctx", clockwise)
                total = total + partial(far, last_cw, 0)
        return total

    def earlier_blocks(key_value, me):
        if n % 2 or n < 4 or REACH != 4:
            return [shifted(key_value, "ctx", by) for by in range(1, REACH)]
        two_back = shifted(key_value, "ctx", 2)
        to_odd = lax.ppermute(
            jnp.stack([key_value, two_back]), "ctx", [(e, e + 1) for e in range(0, n, 2)]
        )
        to_even = lax.ppermute(two_back, "ctx", [(o, o - 1) for o in range(1, n, 2)])
        three_back = lax.ppermute(to_even, "ctx", [(e, (e + 2) % n) for e in range(0, n, 2)])
        odd = (me % 2) == 1
        one_back = jnp.where(odd, to_odd[0], to_even)
        three_back = jnp.where(odd, to_odd[1], three_back)
        return [one_back, two_back, three_back]

    def on_device(tokens, qkv_weight):
        features = lax.all_gather(tokens, "mp", axis=1, tiled=True)
        rows_dev = features.shape[0]
        heads_local = qkv_weight.shape[2]
        head_size = qkv_weight.shape[3]
        scale = 1.0 / math.sqrt(head_size)
        me = lax.axis_index("ctx")

        kv_total = ring_project(features, qkv_weight[:, 1:], me)
        key_value = kv_total.astype(jnp.bfloat16).reshape(rows_dev, 2, heads_local, head_size)
        q_piece, key_value = lax.optimization_barrier((qkv_weight[:, 0], key_value))
        blocks = [key_value] + earlier_blocks(key_value, me)
        q_total = ring_project(features, q_piece, me)
        queries = q_total.astype(jnp.bfloat16).reshape(rows_dev, heads_local, head_size)

        return windowed_attention(queries, blocks, scale)

    return on_device


def solution(mesh):
    placed = (P("ctx", "mp"), P("ctx", None, "mp", None))
    return jax.shard_map(
        make_on_device(ring_order(mesh)),
        mesh=mesh,
        in_specs=placed,
        out_specs=P("ctx", "mp", None),
        check_vma=False,
    )
```

```python
import functools
import math

import jax
import jax.numpy as jnp
from jax import lax
from jax.experimental import pallas as pl
from jax.experimental.pallas import tpu as pltpu
from jax.sharding import PartitionSpec as P

REACH = 4


def attention_kernel(scale, reach, q_ref, *refs):
    k_refs = refs[:reach]
    v_refs = refs[reach : 2 * reach]
    o_ref = refs[2 * reach]
    q = q_ref[...]
    scores = [
        lax.dot_general(q, k_ref[...], (((0,), (0,)), ((), ())), preferred_element_type=jnp.float32) * scale
        for k_ref in k_refs
    ]
    top = scores[0].max(axis=-1, keepdims=True)
    for s in scores[1:]:
        top = jnp.maximum(top, s.max(axis=-1, keepdims=True))
    expos = [jnp.exp(s - top) for s in scores]
    totals = expos[0].sum(axis=-1, keepdims=True)
    for e in expos[1:]:
        totals = totals + e.sum(axis=-1, keepdims=True)
    mixed = None
    for e, v_ref in zip(expos, v_refs):
        term = lax.dot_general(
            e.astype(jnp.bfloat16), v_ref[...], (((1,), (1,)), ((), ())), preferred_element_type=jnp.float32
        )
        mixed = term if mixed is None else mixed + term
    o_ref[0] = (mixed / totals).astype(o_ref.dtype)


def windowed_attention(queries, blocks, scale):
    rows, heads, size = queries.shape
    reach = len(blocks)
    q_t = queries.reshape(rows, heads * size).T
    kv_t = [block.reshape(rows, 2 * heads * size).T for block in blocks]
    q_spec = pl.BlockSpec((size, rows), lambda h: (h, 0))
    v_spec = pl.BlockSpec((size, rows), lambda h: (h + heads, 0))
    keys = rows * reach
    cost = pl.CostEstimate(
        flops=4 * rows * keys * size * heads,
        transcendentals=rows * keys * heads,
        bytes_accessed=2 * (2 * rows * heads * size + 2 * keys * heads * size),
    )
    out = pl.pallas_call(
        functools.partial(attention_kernel, scale, reach),
        out_shape=jax.ShapeDtypeStruct((heads, rows, size), jnp.bfloat16),
        grid=(heads,),
        in_specs=[q_spec] + [q_spec] * reach + [v_spec] * reach,
        out_specs=pl.BlockSpec((1, rows, size), lambda h: (h, 0, 0)),
        cost_estimate=cost,
    )(q_t, *kv_t, *kv_t)
    return jnp.transpose(out, (1, 0, 2))


def ring_order(mesh):
    n = mesh.shape["ctx"]
    order = list(range(n))
    try:
        axis = mesh.axis_names.index("ctx")
        devices = mesh.devices.transpose([axis] + [a for a in range(mesh.devices.ndim) if a != axis])
        devices = devices.reshape(n, -1)[:, 0]
        coords = [tuple(d.coords) for d in devices]
    except Exception:
        return order
    if len(set(coords)) != n:
        return order

    def near(a, b):
        return sum(abs(i - j) for i, j in zip(coords[a], coords[b])) == 1

    neighbours = [[b for b in range(n) if b != a and near(a, b)] for a in range(n)]
    path, seen, budget = [0], {0}, [20000]

    def search():
        budget[0] -= 1
        if budget[0] < 0:
            return False
        if len(path) == n:
            return near(path[-1], path[0]) or n <= 2
        for b in sorted(neighbours[path[-1]], key=lambda b: len([x for x in neighbours[b] if x not in seen])):
            if b in seen:
                continue
            path.append(b)
            seen.add(b)
            if search():
                return True
            path.pop()
            seen.discard(b)
        return False

    if search():
        return path
    return order


def shifted(array, axis, by):
    devices = lax.axis_size(axis)
    return lax.ppermute(array, axis, [(i, (i + by) % devices) for i in range(devices)])


def make_on_device(ring):
    n = len(ring)
    pos = [0] * n
    for i, c in enumerate(ring):
        pos[c] = i
    clockwise = [(ring[i], ring[(i + 1) % n]) for i in range(n)]
    counter = [(ring[i], ring[(i - 1) % n]) for i in range(n)]
    ring_arr = jnp.array(ring, jnp.int32)
    pos_arr = jnp.array(pos, jnp.int32)

    def ring_project(features, piece, me):
        rows_w = piece.shape[0]
        my_pos = pos_arr[me]

        def partial(block, part, offset):
            start = block * rows_w + offset
            cols = lax.dynamic_slice_in_dim(features, start, part.shape[0], axis=1)
            flat = part.reshape(part.shape[0], -1)
            return jnp.dot(cols, flat, preferred_element_type=jnp.float32)

        total = partial(me, piece, 0)
        going_cw = piece
        going_ccw = piece
        for step in range(1, (n - 1) // 2 + 1):
            going_cw = lax.ppermute(going_cw, "ctx", clockwise)
            going_ccw = lax.ppermute(going_ccw, "ctx", counter)
            total = total + partial(ring_arr[(my_pos - step) % n], going_cw, 0)
            total = total + partial(ring_arr[(my_pos + step) % n], going_ccw, 0)
        if n % 2 == 0 and n > 1:
            far = ring_arr[(my_pos + n // 2) % n]
            if rows_w % 2 == 0:
                half = rows_w // 2
                last_cw = lax.ppermute(going_cw[:half], "ctx", clockwise)
                last_ccw = lax.ppermute(going_ccw[half:], "ctx", counter)
                total = total + partial(far, last_cw, 0)
                total = total + partial(far, last_ccw, half)
                return total, (last_cw, last_ccw)
            last_cw = lax.ppermute(going_cw, "ctx", clockwise)
            total = total + partial(far, last_cw, 0)
            return total, (last_cw,)
        return total, (going_cw, going_ccw)

    def earlier_blocks(key_value, me):
        if n % 2 or n < 4 or REACH != 4:
            return [shifted(key_value, "ctx", by) for by in range(1, REACH)]
        two_back = shifted(key_value, "ctx", 2)
        to_odd = lax.ppermute(
            jnp.stack([key_value, two_back]), "ctx", [(e, e + 1) for e in range(0, n, 2)]
        )
        to_even = lax.ppermute(two_back, "ctx", [(o, o - 1) for o in range(1, n, 2)])
        three_back = lax.ppermute(to_even, "ctx", [(e, (e + 2) % n) for e in range(0, n, 2)])
        odd = (me % 2) == 1
        one_back = jnp.where(odd, to_odd[0], to_even)
        three_back = jnp.where(odd, to_odd[1], three_back)
        return [one_back, two_back, three_back]

    def on_device(tokens, qkv_weight):
        features = lax.all_gather(tokens, "mp", axis=1, tiled=True)
        rows_dev = features.shape[0]
        heads_local = qkv_weight.shape[2]
        head_size = qkv_weight.shape[3]
        scale = 1.0 / math.sqrt(head_size)
        me = lax.axis_index("ctx")

        kv_total, arrived = ring_project(features, qkv_weight[:, 1:], me)
        key_value = kv_total.astype(jnp.bfloat16).reshape(rows_dev, 2, heads_local, head_size)
        if n <= 8:
            q_piece, _ = lax.optimization_barrier((qkv_weight[:, 0], arrived))
        else:
            q_piece, key_value = lax.optimization_barrier((qkv_weight[:, 0], key_value))
        blocks = [key_value] + earlier_blocks(key_value, me)
        q_total, _ = ring_project(features, q_piece, me)
        queries = q_total.astype(jnp.bfloat16).reshape(rows_dev, heads_local, head_size)

        return windowed_attention(queries, blocks, scale)

    return on_device


def solution(mesh):
    placed = (P("ctx", "mp"), P("ctx", None, "mp", None))
    return jax.shard_map(
        make_on_device(ring_order(mesh)),
        mesh=mesh,
        in_specs=placed,
        out_specs=P("ctx", "mp", None),
        check_vma=False,
    )
```

```python
import functools
import math

import jax
import jax.numpy as jnp
from jax import lax
from jax.experimental import pallas as pl
from jax.experimental.pallas import tpu as pltpu
from jax.sharding import PartitionSpec as P

REACH = 4


def attention_kernel(scale, reach, q_ref, *refs):
    k_refs = refs[:reach]
    v_refs = refs[reach : 2 * reach]
    o_ref = refs[2 * reach]
    q = q_ref[...].T
    scores = [jnp.dot(q, k_ref[...], preferred_element_type=jnp.float32) * scale for k_ref in k_refs]
    top = scores[0].max(axis=-1, keepdims=True)
    for s in scores[1:]:
        top = jnp.maximum(top, s.max(axis=-1, keepdims=True))
    expos = [jnp.exp(s - top) for s in scores]
    totals = expos[0].sum(axis=-1, keepdims=True)
    for e in expos[1:]:
        totals = totals + e.sum(axis=-1, keepdims=True)
    mixed = None
    for e, v_ref in zip(expos, v_refs):
        term = lax.dot_general(
            e.astype(jnp.bfloat16), v_ref[...], (((1,), (1,)), ((), ())), preferred_element_type=jnp.float32
        )
        mixed = term if mixed is None else mixed + term
    o_ref[0] = (mixed / totals).astype(o_ref.dtype)


def windowed_attention(queries, blocks, scale):
    rows, heads, size = queries.shape
    reach = len(blocks)
    q_t = queries.reshape(rows, heads * size).T
    kv_t = [block.reshape(rows, 2 * heads * size).T for block in blocks]
    q_spec = pl.BlockSpec((size, rows), lambda h: (h, 0))
    v_spec = pl.BlockSpec((size, rows), lambda h: (h + heads, 0))
    keys = rows * reach
    cost = pl.CostEstimate(
        flops=4 * rows * keys * size * heads,
        transcendentals=rows * keys * heads,
        bytes_accessed=2 * (2 * rows * heads * size + 2 * keys * heads * size),
    )
    out = pl.pallas_call(
        functools.partial(attention_kernel, scale, reach),
        out_shape=jax.ShapeDtypeStruct((heads, rows, size), jnp.bfloat16),
        grid=(heads,),
        in_specs=[q_spec] + [q_spec] * reach + [v_spec] * reach,
        out_specs=pl.BlockSpec((1, rows, size), lambda h: (h, 0, 0)),
        cost_estimate=cost,
    )(q_t, *kv_t, *kv_t)
    return jnp.transpose(out, (1, 0, 2))


def ring_order(mesh):
    n = mesh.shape["ctx"]
    order = list(range(n))
    try:
        axis = mesh.axis_names.index("ctx")
        devices = mesh.devices.transpose([axis] + [a for a in range(mesh.devices.ndim) if a != axis])
        devices = devices.reshape(n, -1)[:, 0]
        coords = [tuple(d.coords) for d in devices]
    except Exception:
        return order
    if len(set(coords)) != n:
        return order

    def near(a, b):
        return sum(abs(i - j) for i, j in zip(coords[a], coords[b])) == 1

    neighbours = [[b for b in range(n) if b != a and near(a, b)] for a in range(n)]
    path, seen, budget = [0], {0}, [20000]

    def search():
        budget[0] -= 1
        if budget[0] < 0:
            return False
        if len(path) == n:
            return near(path[-1], path[0]) or n <= 2
        for b in sorted(neighbours[path[-1]], key=lambda b: len([x for x in neighbours[b] if x not in seen])):
            if b in seen:
                continue
            path.append(b)
            seen.add(b)
            if search():
                return True
            path.pop()
            seen.discard(b)
        return False

    if search():
        return path
    return order


def shifted(array, axis, by):
    devices = lax.axis_size(axis)
    return lax.ppermute(array, axis, [(i, (i + by) % devices) for i in range(devices)])


def make_on_device(ring):
    n = len(ring)
    pos = [0] * n
    for i, c in enumerate(ring):
        pos[c] = i
    clockwise = [(ring[i], ring[(i + 1) % n]) for i in range(n)]
    counter = [(ring[i], ring[(i - 1) % n]) for i in range(n)]
    ring_arr = jnp.array(ring, jnp.int32)
    pos_arr = jnp.array(pos, jnp.int32)

    def ring_project(features, piece, me):
        rows_w = piece.shape[0]
        my_pos = pos_arr[me]

        def partial(block, part, offset):
            start = block * rows_w + offset
            cols = lax.dynamic_slice_in_dim(features, start, part.shape[0], axis=1)
            flat = part.reshape(part.shape[0], -1)
            return jnp.dot(cols, flat, preferred_element_type=jnp.float32)

        total = partial(me, piece, 0)
        going_cw = piece
        going_ccw = piece
        for step in range(1, (n - 1) // 2 + 1):
            going_cw = lax.ppermute(going_cw, "ctx", clockwise)
            going_ccw = lax.ppermute(going_ccw, "ctx", counter)
            total = total + partial(ring_arr[(my_pos - step) % n], going_cw, 0)
            total = total + partial(ring_arr[(my_pos + step) % n], going_ccw, 0)
        if n % 2 == 0 and n > 1:
            far = ring_arr[(my_pos + n // 2) % n]
            if rows_w % 2 == 0:
                half = rows_w // 2
                last_cw = lax.ppermute(going_cw[:half], "ctx", clockwise)
                last_ccw = lax.ppermute(going_ccw[half:], "ctx", counter)
                total = total + partial(far, last_cw, 0)
                total = total + partial(far, last_ccw, half)
                return total, (last_cw, last_ccw)
            last_cw = lax.ppermute(going_cw, "ctx", clockwise)
            total = total + partial(far, last_cw, 0)
            return total, (last_cw,)
        return total, (going_cw, going_ccw)

    def earlier_blocks(key_value, me):
        if n % 2 or n < 4 or REACH != 4:
            return [shifted(key_value, "ctx", by) for by in range(1, REACH)]
        two_back = shifted(key_value, "ctx", 2)
        to_odd = lax.ppermute(
            jnp.stack([key_value, two_back]), "ctx", [(e, e + 1) for e in range(0, n, 2)]
        )
        to_even = lax.ppermute(two_back, "ctx", [(o, o - 1) for o in range(1, n, 2)])
        three_back = lax.ppermute(to_even, "ctx", [(e, (e + 2) % n) for e in range(0, n, 2)])
        odd = (me % 2) == 1
        one_back = jnp.where(odd, to_odd[0], to_even)
        three_back = jnp.where(odd, to_odd[1], three_back)
        return [one_back, two_back, three_back]

    def on_device(tokens, qkv_weight):
        features = lax.all_gather(tokens, "mp", axis=1, tiled=True)
        rows_dev = features.shape[0]
        heads_local = qkv_weight.shape[2]
        head_size = qkv_weight.shape[3]
        scale = 1.0 / math.sqrt(head_size)
        me = lax.axis_index("ctx")

        kv_total, arrived = ring_project(features, qkv_weight[:, 1:], me)
        key_value = kv_total.astype(jnp.bfloat16).reshape(rows_dev, 2, heads_local, head_size)
        if n <= 8:
            q_piece, _ = lax.optimization_barrier((qkv_weight[:, 0], arrived))
        else:
            q_piece, key_value = lax.optimization_barrier((qkv_weight[:, 0], key_value))
        blocks = [key_value] + earlier_blocks(key_value, me)
        q_total, _ = ring_project(features, q_piece, me)
        queries = q_total.astype(jnp.bfloat16).reshape(rows_dev, heads_local, head_size)

        return windowed_attention(queries, blocks, scale)

    return on_device


def solution(mesh):
    placed = (P("ctx", "mp"), P("ctx", None, "mp", None))
    return jax.shard_map(
        make_on_device(ring_order(mesh)),
        mesh=mesh,
        in_specs=placed,
        out_specs=P("ctx", "mp", None),
        check_vma=False,
    )
```

```python
import functools
import math

import jax
import jax.numpy as jnp
from jax import lax
from jax.experimental import pallas as pl
from jax.experimental.pallas import tpu as pltpu
from jax.sharding import PartitionSpec as P

REACH = 4


def attention_kernel(scale, reach, q_ref, *refs):
    k_refs = refs[:reach]
    v_refs = refs[reach : 2 * reach]
    o_ref = refs[2 * reach]
    q = q_ref[...].T
    scores = [jnp.dot(q, k_ref[...], preferred_element_type=jnp.float32) * scale for k_ref in k_refs]
    top = scores[0].max(axis=-1, keepdims=True)
    for s in scores[1:]:
        top = jnp.maximum(top, s.max(axis=-1, keepdims=True))
    expos = [jnp.exp(s - top) for s in scores]
    totals = expos[0].sum(axis=-1, keepdims=True)
    for e in expos[1:]:
        totals = totals + e.sum(axis=-1, keepdims=True)
    mixed = None
    for e, v_ref in zip(expos, v_refs):
        term = lax.dot_general(
            e.astype(jnp.bfloat16), v_ref[...], (((1,), (1,)), ((), ())), preferred_element_type=jnp.float32
        )
        mixed = term if mixed is None else mixed + term
    o_ref[0] = (mixed / totals).astype(o_ref.dtype)


def windowed_attention(queries, blocks, scale):
    rows, heads, size = queries.shape
    reach = len(blocks)
    q_t = queries.reshape(rows, heads * size).T
    kv_t = [block.reshape(rows, 2 * heads * size).T for block in blocks]
    q_spec = pl.BlockSpec((size, rows), lambda h: (h, 0))
    v_spec = pl.BlockSpec((size, rows), lambda h: (h + heads, 0))
    keys = rows * reach
    cost = pl.CostEstimate(
        flops=4 * rows * keys * size * heads,
        transcendentals=rows * keys * heads,
        bytes_accessed=2 * (2 * rows * heads * size + 2 * keys * heads * size),
    )
    out = pl.pallas_call(
        functools.partial(attention_kernel, scale, reach),
        out_shape=jax.ShapeDtypeStruct((heads, rows, size), jnp.bfloat16),
        grid=(heads,),
        in_specs=[q_spec] + [q_spec] * reach + [v_spec] * reach,
        out_specs=pl.BlockSpec((1, rows, size), lambda h: (h, 0, 0)),
        cost_estimate=cost,
    )(q_t, *kv_t, *kv_t)
    return jnp.transpose(out, (1, 0, 2))


def ring_order(mesh):
    n = mesh.shape["ctx"]
    order = list(range(n))
    try:
        axis = mesh.axis_names.index("ctx")
        devices = mesh.devices.transpose([axis] + [a for a in range(mesh.devices.ndim) if a != axis])
        devices = devices.reshape(n, -1)[:, 0]
        coords = [tuple(d.coords) for d in devices]
    except Exception:
        return order
    if len(set(coords)) != n:
        return order

    def near(a, b):
        return sum(abs(i - j) for i, j in zip(coords[a], coords[b])) == 1

    neighbours = [[b for b in range(n) if b != a and near(a, b)] for a in range(n)]
    path, seen, budget = [0], {0}, [20000]

    def search():
        budget[0] -= 1
        if budget[0] < 0:
            return False
        if len(path) == n:
            return near(path[-1], path[0]) or n <= 2
        for b in sorted(neighbours[path[-1]], key=lambda b: len([x for x in neighbours[b] if x not in seen])):
            if b in seen:
                continue
            path.append(b)
            seen.add(b)
            if search():
                return True
            path.pop()
            seen.discard(b)
        return False

    if search():
        return path
    return order


def shifted(array, axis, by):
    devices = lax.axis_size(axis)
    return lax.ppermute(array, axis, [(i, (i + by) % devices) for i in range(devices)])


def make_on_device(ring):
    n = len(ring)
    pos = [0] * n
    for i, c in enumerate(ring):
        pos[c] = i
    clockwise = [(ring[i], ring[(i + 1) % n]) for i in range(n)]
    counter = [(ring[i], ring[(i - 1) % n]) for i in range(n)]
    ring_arr = jnp.array(ring, jnp.int32)
    pos_arr = jnp.array(pos, jnp.int32)

    def ring_project(features, piece, me):
        rows_w = piece.shape[0]
        my_pos = pos_arr[me]

        def partial(block, part, offset):
            start = block * rows_w + offset
            cols = lax.dynamic_slice_in_dim(features, start, part.shape[0], axis=1)
            flat = part.reshape(part.shape[0], -1)
            return jnp.dot(cols, flat, preferred_element_type=jnp.float32)

        total = partial(me, piece, 0)
        going_cw = piece
        going_ccw = piece
        for step in range(1, (n - 1) // 2 + 1):
            going_cw = lax.ppermute(going_cw, "ctx", clockwise)
            going_ccw = lax.ppermute(going_ccw, "ctx", counter)
            total = total + partial(ring_arr[(my_pos - step) % n], going_cw, 0)
            total = total + partial(ring_arr[(my_pos + step) % n], going_ccw, 0)
        if n % 2 == 0 and n > 1:
            far = ring_arr[(my_pos + n // 2) % n]
            if rows_w % 2 == 0:
                half = rows_w // 2
                last_cw = lax.ppermute(going_cw[:half], "ctx", clockwise)
                last_ccw = lax.ppermute(going_ccw[half:], "ctx", counter)
                total = total + partial(far, last_cw, 0)
                total = total + partial(far, last_ccw, half)
                return total, (last_cw, last_ccw)
            last_cw = lax.ppermute(going_cw, "ctx", clockwise)
            total = total + partial(far, last_cw, 0)
            return total, (last_cw,)
        return total, (going_cw, going_ccw)

    def earlier_blocks(key_value, me):
        if n % 2 or n < 4 or REACH != 4:
            return [shifted(key_value, "ctx", by) for by in range(1, REACH)]
        two_back = shifted(key_value, "ctx", 2)
        evens_up = [(e, e + 1) for e in range(0, n, 2)]
        own_up = lax.ppermute(key_value, "ctx", evens_up)
        two_back_up = lax.ppermute(two_back, "ctx", evens_up)
        to_even = lax.ppermute(two_back, "ctx", [(o, o - 1) for o in range(1, n, 2)])
        three_back = lax.ppermute(to_even, "ctx", [(e, (e + 2) % n) for e in range(0, n, 2)])
        odd = (me % 2) == 1
        one_back = jnp.where(odd, own_up, to_even)
        three_back = jnp.where(odd, two_back_up, three_back)
        return [one_back, two_back, three_back]

    def on_device(tokens, qkv_weight):
        features = lax.all_gather(tokens, "mp", axis=1, tiled=True)
        rows_dev = features.shape[0]
        heads_local = qkv_weight.shape[2]
        head_size = qkv_weight.shape[3]
        scale = 1.0 / math.sqrt(head_size)
        me = lax.axis_index("ctx")

        kv_total, arrived = ring_project(features, qkv_weight[:, 1:], me)
        key_value = kv_total.astype(jnp.bfloat16).reshape(rows_dev, 2, heads_local, head_size)
        if n <= 8:
            q_piece, _ = lax.optimization_barrier((qkv_weight[:, 0], arrived))
        else:
            q_piece, key_value = lax.optimization_barrier((qkv_weight[:, 0], key_value))
        blocks = [key_value] + earlier_blocks(key_value, me)
        q_total, _ = ring_project(features, q_piece, me)
        queries = q_total.astype(jnp.bfloat16).reshape(rows_dev, heads_local, head_size)

        return windowed_attention(queries, blocks, scale)

    return on_device


def solution(mesh):
    placed = (P("ctx", "mp"), P("ctx", None, "mp", None))
    return jax.shard_map(
        make_on_device(ring_order(mesh)),
        mesh=mesh,
        in_specs=placed,
        out_specs=P("ctx", "mp", None),
        check_vma=False,
    )
```

```python
import functools
import math

import jax
import jax.numpy as jnp
from jax import lax
from jax.experimental import pallas as pl
from jax.experimental.pallas import tpu as pltpu
from jax.sharding import PartitionSpec as P

REACH = 4


def attention_kernel(scale, reach, q_ref, *refs):
    k_refs = refs[:reach]
    v_refs = refs[reach : 2 * reach]
    o_ref = refs[2 * reach]
    q = q_ref[...].T
    scores = [jnp.dot(q, k_ref[...], preferred_element_type=jnp.float32) * scale for k_ref in k_refs]
    top = scores[0].max(axis=-1, keepdims=True)
    for s in scores[1:]:
        top = jnp.maximum(top, s.max(axis=-1, keepdims=True))
    expos = [jnp.exp(s - top) for s in scores]
    totals = expos[0].sum(axis=-1, keepdims=True)
    for e in expos[1:]:
        totals = totals + e.sum(axis=-1, keepdims=True)
    mixed = None
    for e, v_ref in zip(expos, v_refs):
        term = lax.dot_general(
            e.astype(jnp.bfloat16), v_ref[...], (((1,), (1,)), ((), ())), preferred_element_type=jnp.float32
        )
        mixed = term if mixed is None else mixed + term
    o_ref[0] = (mixed / totals).astype(o_ref.dtype)


def windowed_attention(queries, blocks, scale):
    rows, heads, size = queries.shape
    reach = len(blocks)
    q_t = queries.reshape(rows, heads * size).T
    kv_t = [block.reshape(rows, 2 * heads * size).T for block in blocks]
    q_spec = pl.BlockSpec((size, rows), lambda h: (h, 0))
    v_spec = pl.BlockSpec((size, rows), lambda h: (h + heads, 0))
    keys = rows * reach
    cost = pl.CostEstimate(
        flops=4 * rows * keys * size * heads,
        transcendentals=rows * keys * heads,
        bytes_accessed=2 * (2 * rows * heads * size + 2 * keys * heads * size),
    )
    out = pl.pallas_call(
        functools.partial(attention_kernel, scale, reach),
        out_shape=jax.ShapeDtypeStruct((heads, rows, size), jnp.bfloat16),
        grid=(heads,),
        in_specs=[q_spec] + [q_spec] * reach + [v_spec] * reach,
        out_specs=pl.BlockSpec((1, rows, size), lambda h: (h, 0, 0)),
        cost_estimate=cost,
    )(q_t, *kv_t, *kv_t)
    return jnp.transpose(out, (1, 0, 2))


def ring_order(mesh):
    n = mesh.shape["ctx"]
    order = list(range(n))
    try:
        axis = mesh.axis_names.index("ctx")
        devices = mesh.devices.transpose([axis] + [a for a in range(mesh.devices.ndim) if a != axis])
        devices = devices.reshape(n, -1)[:, 0]
        coords = [tuple(d.coords) for d in devices]
    except Exception:
        return order
    if len(set(coords)) != n:
        return order

    def near(a, b):
        return sum(abs(i - j) for i, j in zip(coords[a], coords[b])) == 1

    neighbours = [[b for b in range(n) if b != a and near(a, b)] for a in range(n)]
    path, seen, budget = [0], {0}, [20000]

    def search():
        budget[0] -= 1
        if budget[0] < 0:
            return False
        if len(path) == n:
            return near(path[-1], path[0]) or n <= 2
        for b in sorted(neighbours[path[-1]], key=lambda b: len([x for x in neighbours[b] if x not in seen])):
            if b in seen:
                continue
            path.append(b)
            seen.add(b)
            if search():
                return True
            path.pop()
            seen.discard(b)
        return False

    if search():
        return path
    return order


def shifted(array, axis, by):
    devices = lax.axis_size(axis)
    return lax.ppermute(array, axis, [(i, (i + by) % devices) for i in range(devices)])


def make_on_device(ring):
    n = len(ring)
    pos = [0] * n
    for i, c in enumerate(ring):
        pos[c] = i
    clockwise = [(ring[i], ring[(i + 1) % n]) for i in range(n)]
    counter = [(ring[i], ring[(i - 1) % n]) for i in range(n)]
    ring_arr = jnp.array(ring, jnp.int32)
    pos_arr = jnp.array(pos, jnp.int32)

    def ring_project(features, piece, me):
        rows_w = piece.shape[0]
        my_pos = pos_arr[me]

        def partial(block, part, offset):
            start = block * rows_w + offset
            cols = lax.dynamic_slice_in_dim(features, start, part.shape[0], axis=1)
            flat = part.reshape(part.shape[0], -1)
            return jnp.dot(cols, flat, preferred_element_type=jnp.float32)

        total = partial(me, piece, 0)
        going_cw = piece
        going_ccw = piece
        for step in range(1, (n - 1) // 2 + 1):
            going_cw = lax.ppermute(going_cw, "ctx", clockwise)
            going_ccw = lax.ppermute(going_ccw, "ctx", counter)
            total = total + partial(ring_arr[(my_pos - step) % n], going_cw, 0)
            total = total + partial(ring_arr[(my_pos + step) % n], going_ccw, 0)
        if n % 2 == 0 and n > 1:
            far = ring_arr[(my_pos + n // 2) % n]
            if rows_w % 2 == 0:
                half = rows_w // 2
                last_cw = lax.ppermute(going_cw[:half], "ctx", clockwise)
                last_ccw = lax.ppermute(going_ccw[half:], "ctx", counter)
                total = total + partial(far, last_cw, 0)
                total = total + partial(far, last_ccw, half)
                return total, (last_cw, last_ccw)
            last_cw = lax.ppermute(going_cw, "ctx", clockwise)
            total = total + partial(far, last_cw, 0)
            return total, (last_cw,)
        return total, (going_cw, going_ccw)

    def earlier_blocks(key_value, me):
        if n % 2 or n < 4 or REACH != 4:
            return [shifted(key_value, "ctx", by) for by in range(1, REACH)]
        two_back = shifted(key_value, "ctx", 2)
        evens_up = [(e, e + 1) for e in range(0, n, 2)]
        own_up = lax.ppermute(key_value, "ctx", evens_up)
        two_back_up = lax.ppermute(two_back, "ctx", evens_up)
        to_even = lax.ppermute(two_back, "ctx", [(o, o - 1) for o in range(1, n, 2)])
        three_back = lax.ppermute(to_even, "ctx", [(e, (e + 2) % n) for e in range(0, n, 2)])
        odd = (me % 2) == 1
        one_back = jnp.where(odd, own_up, to_even)
        three_back = jnp.where(odd, two_back_up, three_back)
        return [one_back, two_back, three_back]

    def on_device(tokens, qkv_weight):
        parts = lax.axis_size("mp")
        me_mp = lax.axis_index("mp")
        width = tokens.shape[1]
        features = jnp.zeros((tokens.shape[0], width * parts), tokens.dtype)
        features = lax.dynamic_update_slice(features, tokens, (0, me_mp * width))
        for by in range(1, parts):
            piece = shifted(tokens, "mp", by)
            features = lax.dynamic_update_slice(features, piece, (0, ((me_mp - by) % parts) * width))
        rows_dev = features.shape[0]
        heads_local = qkv_weight.shape[2]
        head_size = qkv_weight.shape[3]
        scale = 1.0 / math.sqrt(head_size)
        me = lax.axis_index("ctx")

        kv_total, arrived = ring_project(features, qkv_weight[:, 1:], me)
        key_value = kv_total.astype(jnp.bfloat16).reshape(rows_dev, 2, heads_local, head_size)
        if n <= 8:
            q_piece, _ = lax.optimization_barrier((qkv_weight[:, 0], arrived))
        else:
            q_piece, key_value = lax.optimization_barrier((qkv_weight[:, 0], key_value))
        blocks = [key_value] + earlier_blocks(key_value, me)
        q_total, _ = ring_project(features, q_piece, me)
        queries = q_total.astype(jnp.bfloat16).reshape(rows_dev, heads_local, head_size)

        return windowed_attention(queries, blocks, scale)

    return on_device


def solution(mesh):
    placed = (P("ctx", "mp"), P("ctx", None, "mp", None))
    return jax.shard_map(
        make_on_device(ring_order(mesh)),
        mesh=mesh,
        in_specs=placed,
        out_specs=P("ctx", "mp", None),
        check_vma=False,
    )
```

```python
import functools
import math

import jax
import jax.numpy as jnp
from jax import lax
from jax.experimental import pallas as pl
from jax.experimental.pallas import tpu as pltpu
from jax.sharding import PartitionSpec as P

REACH = 4


def attention_kernel(scale, reach, q_ref, *refs):
    k_refs = refs[:reach]
    v_refs = refs[reach : 2 * reach]
    o_ref = refs[2 * reach]
    q = q_ref[...].T
    scores = [jnp.dot(q, k_ref[...], preferred_element_type=jnp.float32) * scale for k_ref in k_refs]
    top = scores[0].max(axis=-1, keepdims=True)
    for s in scores[1:]:
        top = jnp.maximum(top, s.max(axis=-1, keepdims=True))
    expos = [jnp.exp(s - top) for s in scores]
    totals = expos[0].sum(axis=-1, keepdims=True)
    for e in expos[1:]:
        totals = totals + e.sum(axis=-1, keepdims=True)
    mixed = None
    for e, v_ref in zip(expos, v_refs):
        term = lax.dot_general(
            e.astype(jnp.bfloat16), v_ref[...], (((1,), (1,)), ((), ())), preferred_element_type=jnp.float32
        )
        mixed = term if mixed is None else mixed + term
    o_ref[0] = (mixed / totals).astype(o_ref.dtype)


def windowed_attention(queries, blocks, scale):
    rows, heads, size = queries.shape
    reach = len(blocks)
    q_t = queries.reshape(rows, heads * size).T
    kv_t = [block.reshape(rows, 2 * heads * size).T for block in blocks]
    q_spec = pl.BlockSpec((size, rows), lambda h: (h, 0))
    v_spec = pl.BlockSpec((size, rows), lambda h: (h + heads, 0))
    keys = rows * reach
    cost = pl.CostEstimate(
        flops=4 * rows * keys * size * heads,
        transcendentals=rows * keys * heads,
        bytes_accessed=2 * (2 * rows * heads * size + 2 * keys * heads * size),
    )
    out = pl.pallas_call(
        functools.partial(attention_kernel, scale, reach),
        out_shape=jax.ShapeDtypeStruct((heads, rows, size), jnp.bfloat16),
        grid=(heads,),
        in_specs=[q_spec] + [q_spec] * reach + [v_spec] * reach,
        out_specs=pl.BlockSpec((1, rows, size), lambda h: (h, 0, 0)),
        cost_estimate=cost,
    )(q_t, *kv_t, *kv_t)
    return jnp.transpose(out, (1, 0, 2))


def ring_order(mesh):
    n = mesh.shape["ctx"]
    order = list(range(n))
    try:
        axis = mesh.axis_names.index("ctx")
        devices = mesh.devices.transpose([axis] + [a for a in range(mesh.devices.ndim) if a != axis])
        devices = devices.reshape(n, -1)[:, 0]
        coords = [tuple(d.coords) for d in devices]
    except Exception:
        return order
    if len(set(coords)) != n:
        return order

    def near(a, b):
        return sum(abs(i - j) for i, j in zip(coords[a], coords[b])) == 1

    neighbours = [[b for b in range(n) if b != a and near(a, b)] for a in range(n)]
    path, seen, budget = [0], {0}, [20000]

    def search():
        budget[0] -= 1
        if budget[0] < 0:
            return False
        if len(path) == n:
            return near(path[-1], path[0]) or n <= 2
        for b in sorted(neighbours[path[-1]], key=lambda b: len([x for x in neighbours[b] if x not in seen])):
            if b in seen:
                continue
            path.append(b)
            seen.add(b)
            if search():
                return True
            path.pop()
            seen.discard(b)
        return False

    if search():
        return path
    return order


def shifted(array, axis, by):
    devices = lax.axis_size(axis)
    return lax.ppermute(array, axis, [(i, (i + by) % devices) for i in range(devices)])


def make_on_device(ring):
    n = len(ring)
    pos = [0] * n
    for i, c in enumerate(ring):
        pos[c] = i
    clockwise = [(ring[i], ring[(i + 1) % n]) for i in range(n)]
    counter = [(ring[i], ring[(i - 1) % n]) for i in range(n)]
    ring_arr = jnp.array(ring, jnp.int32)
    head_major = n <= 8
    pos_arr = jnp.array(pos, jnp.int32)

    def ring_project(features, piece, me):
        axis = -2 if head_major else 0
        rows_w = piece.shape[axis]
        my_pos = pos_arr[me]

        def partial(block, part, offset):
            start = block * rows_w + offset
            cols = lax.dynamic_slice_in_dim(features, start, part.shape[axis], axis=1)
            if head_major:
                return jnp.einsum("tr,...rd->t...d", cols, part, preferred_element_type=jnp.float32)
            flat = part.reshape(part.shape[0], -1)
            return jnp.dot(cols, flat, preferred_element_type=jnp.float32)

        total = partial(me, piece, 0)
        going_cw = piece
        going_ccw = piece
        for step in range(1, (n - 1) // 2 + 1):
            going_cw = lax.ppermute(going_cw, "ctx", clockwise)
            going_ccw = lax.ppermute(going_ccw, "ctx", counter)
            total = total + partial(ring_arr[(my_pos - step) % n], going_cw, 0)
            total = total + partial(ring_arr[(my_pos + step) % n], going_ccw, 0)
        if n % 2 == 0 and n > 1:
            far = ring_arr[(my_pos + n // 2) % n]
            if rows_w % 2 == 0:
                half = rows_w // 2
                first = lax.slice_in_dim(going_cw, 0, half, axis=axis % going_cw.ndim)
                second = lax.slice_in_dim(going_ccw, half, rows_w, axis=axis % going_ccw.ndim)
                last_cw = lax.ppermute(first, "ctx", clockwise)
                last_ccw = lax.ppermute(second, "ctx", counter)
                total = total + partial(far, last_cw, 0)
                total = total + partial(far, last_ccw, half)
                return total, (last_cw, last_ccw)
            last_cw = lax.ppermute(going_cw, "ctx", clockwise)
            total = total + partial(far, last_cw, 0)
            return total, (last_cw,)
        return total, (going_cw, going_ccw)

    def earlier_blocks(key_value, me):
        if n % 2 or n < 4 or REACH != 4:
            return [shifted(key_value, "ctx", by) for by in range(1, REACH)]
        two_back = shifted(key_value, "ctx", 2)
        evens_up = [(e, e + 1) for e in range(0, n, 2)]
        own_up = lax.ppermute(key_value, "ctx", evens_up)
        two_back_up = lax.ppermute(two_back, "ctx", evens_up)
        to_even = lax.ppermute(two_back, "ctx", [(o, o - 1) for o in range(1, n, 2)])
        three_back = lax.ppermute(to_even, "ctx", [(e, (e + 2) % n) for e in range(0, n, 2)])
        odd = (me % 2) == 1
        one_back = jnp.where(odd, own_up, to_even)
        three_back = jnp.where(odd, two_back_up, three_back)
        return [one_back, two_back, three_back]

    def on_device(tokens, qkv_weight):
        parts = lax.axis_size("mp")
        me_mp = lax.axis_index("mp")
        width = tokens.shape[1]
        features = jnp.zeros((tokens.shape[0], width * parts), tokens.dtype)
        features = lax.dynamic_update_slice(features, tokens, (0, me_mp * width))
        for by in range(1, parts):
            piece = shifted(tokens, "mp", by)
            features = lax.dynamic_update_slice(features, piece, (0, ((me_mp - by) % parts) * width))
        rows_dev = features.shape[0]
        heads_local = qkv_weight.shape[2]
        head_size = qkv_weight.shape[3]
        scale = 1.0 / math.sqrt(head_size)
        me = lax.axis_index("ctx")

        if head_major:
            by_head = jnp.transpose(qkv_weight, (1, 2, 0, 3))
            kv_piece, q_piece = by_head[1:], by_head[0]
        else:
            kv_piece, q_piece = qkv_weight[:, 1:], qkv_weight[:, 0]
        kv_total, arrived = ring_project(features, kv_piece, me)
        key_value = kv_total.astype(jnp.bfloat16).reshape(rows_dev, 2, heads_local, head_size)
        if n <= 8:
            q_piece, _ = lax.optimization_barrier((q_piece, arrived))
        else:
            q_piece, key_value = lax.optimization_barrier((q_piece, key_value))
        blocks = [key_value] + earlier_blocks(key_value, me)
        q_total, _ = ring_project(features, q_piece, me)
        queries = q_total.astype(jnp.bfloat16).reshape(rows_dev, heads_local, head_size)

        return windowed_attention(queries, blocks, scale)

    return on_device


def solution(mesh):
    placed = (P("ctx", "mp"), P("ctx", None, "mp", None))
    return jax.shard_map(
        make_on_device(ring_order(mesh)),
        mesh=mesh,
        in_specs=placed,
        out_specs=P("ctx", "mp", None),
        check_vma=False,
    )
```

```python
import functools
import math

import jax
import jax.numpy as jnp
from jax import lax
from jax.experimental import pallas as pl
from jax.experimental.pallas import tpu as pltpu
from jax.sharding import PartitionSpec as P

REACH = 4


def attention_kernel(scale, reach, q_ref, *refs):
    k_refs = refs[:reach]
    v_refs = refs[reach : 2 * reach]
    o_ref = refs[2 * reach]
    q = q_ref[...].T
    scores = [jnp.dot(q, k_ref[...], preferred_element_type=jnp.float32) * scale for k_ref in k_refs]
    top = scores[0].max(axis=-1, keepdims=True)
    for s in scores[1:]:
        top = jnp.maximum(top, s.max(axis=-1, keepdims=True))
    expos = [jnp.exp(s - top) for s in scores]
    totals = expos[0].sum(axis=-1, keepdims=True)
    for e in expos[1:]:
        totals = totals + e.sum(axis=-1, keepdims=True)
    mixed = None
    for e, v_ref in zip(expos, v_refs):
        term = lax.dot_general(
            e.astype(jnp.bfloat16), v_ref[...], (((1,), (1,)), ((), ())), preferred_element_type=jnp.float32
        )
        mixed = term if mixed is None else mixed + term
    o_ref[0] = (mixed / totals).astype(o_ref.dtype)


def windowed_attention(q_t, kv_t, scale, size):
    rows = q_t.shape[1]
    heads = q_t.shape[0] // size
    reach = len(kv_t)
    q_spec = pl.BlockSpec((size, rows), lambda h: (h, 0))
    v_spec = pl.BlockSpec((size, rows), lambda h: (h + heads, 0))
    keys = rows * reach
    cost = pl.CostEstimate(
        flops=4 * rows * keys * size * heads,
        transcendentals=rows * keys * heads,
        bytes_accessed=2 * (2 * rows * heads * size + 2 * keys * heads * size),
    )
    out = pl.pallas_call(
        functools.partial(attention_kernel, scale, reach),
        out_shape=jax.ShapeDtypeStruct((heads, rows, size), jnp.bfloat16),
        grid=(heads,),
        in_specs=[q_spec] + [q_spec] * reach + [v_spec] * reach,
        out_specs=pl.BlockSpec((1, rows, size), lambda h: (h, 0, 0)),
        cost_estimate=cost,
    )(q_t, *kv_t, *kv_t)
    return jnp.transpose(out, (1, 0, 2))


def accumulate_kernel(block_ref, feat_ref, w_ref, acc_ref, out_ref):
    out_ref[...] = acc_ref[...] + lax.dot_general(
        w_ref[0], feat_ref[...], (((0,), (1,)), ((), ())), preferred_element_type=jnp.float32
    )


def accumulate(total_t, features, part, column_block):
    groups, rows, size = part.shape
    tokens = features.shape[0]
    return pl.pallas_call(
        accumulate_kernel,
        out_shape=jax.ShapeDtypeStruct(total_t.shape, jnp.float32),
        grid_spec=pltpu.PrefetchScalarGridSpec(
            num_scalar_prefetch=1,
            grid=(groups,),
            in_specs=[
                pl.BlockSpec((tokens, rows), lambda g, b: (0, b[0])),
                pl.BlockSpec((1, rows, size), lambda g, b: (g, 0, 0)),
                pl.BlockSpec((size, tokens), lambda g, b: (g, 0)),
            ],
            out_specs=pl.BlockSpec((size, tokens), lambda g, b: (g, 0)),
        ),
        input_output_aliases={3: 0},
        cost_estimate=pl.CostEstimate(
            flops=2 * tokens * rows * groups * size,
            transcendentals=0,
            bytes_accessed=2 * tokens * rows + 2 * groups * rows * size + 8 * groups * size * tokens,
        ),
    )(jnp.reshape(column_block, (1,)).astype(jnp.int32), features, part, total_t)


def ring_order(mesh):
    n = mesh.shape["ctx"]
    order = list(range(n))
    try:
        axis = mesh.axis_names.index("ctx")
        devices = mesh.devices.transpose([axis] + [a for a in range(mesh.devices.ndim) if a != axis])
        devices = devices.reshape(n, -1)[:, 0]
        coords = [tuple(d.coords) for d in devices]
    except Exception:
        return order
    if len(set(coords)) != n:
        return order

    def near(a, b):
        return sum(abs(i - j) for i, j in zip(coords[a], coords[b])) == 1

    neighbours = [[b for b in range(n) if b != a and near(a, b)] for a in range(n)]
    path, seen, budget = [0], {0}, [20000]

    def search():
        budget[0] -= 1
        if budget[0] < 0:
            return False
        if len(path) == n:
            return near(path[-1], path[0]) or n <= 2
        for b in sorted(neighbours[path[-1]], key=lambda b: len([x for x in neighbours[b] if x not in seen])):
            if b in seen:
                continue
            path.append(b)
            seen.add(b)
            if search():
                return True
            path.pop()
            seen.discard(b)
        return False

    if search():
        return path
    return order


def shifted(array, axis, by):
    devices = lax.axis_size(axis)
    return lax.ppermute(array, axis, [(i, (i + by) % devices) for i in range(devices)])


def make_on_device(ring):
    n = len(ring)
    pos = [0] * n
    for i, c in enumerate(ring):
        pos[c] = i
    clockwise = [(ring[i], ring[(i + 1) % n]) for i in range(n)]
    counter = [(ring[i], ring[(i - 1) % n]) for i in range(n)]
    ring_arr = jnp.array(ring, jnp.int32)
    head_major = n <= 8
    pos_arr = jnp.array(pos, jnp.int32)

    def ring_project(features, piece, me):
        axis = -2 if head_major else 0
        rows_w = piece.shape[axis]
        my_pos = pos_arr[me]

        def partial(block, part, offset):
            start = block * rows_w + offset
            cols = lax.dynamic_slice_in_dim(features, start, part.shape[axis], axis=1)
            if head_major:
                return jnp.einsum("tr,...rd->t...d", cols, part, preferred_element_type=jnp.float32)
            flat = part.reshape(part.shape[0], -1)
            return jnp.dot(cols, flat, preferred_element_type=jnp.float32)

        if head_major:
            size = piece.shape[-1]
            piece = piece.reshape(-1, rows_w, size)
            empty = jnp.zeros((piece.shape[0] * size, features.shape[0]), jnp.float32)

            def partial(block, part, offset):
                return lambda total_t: accumulate(
                    total_t, features, part, (block * rows_w + offset) // part.shape[1]
                )

            def combine(total, term):
                return term(total)

            total = combine(empty, partial(me, piece, 0))
        else:
            total = partial(me, piece, 0).T

            def combine(total, term):
                return total + term.T

        going_cw = piece
        going_ccw = piece
        for step in range(1, (n - 1) // 2 + 1):
            going_cw = lax.ppermute(going_cw, "ctx", clockwise)
            going_ccw = lax.ppermute(going_ccw, "ctx", counter)
            total = combine(total, partial(ring_arr[(my_pos - step) % n], going_cw, 0))
            total = combine(total, partial(ring_arr[(my_pos + step) % n], going_ccw, 0))
        if n % 2 == 0 and n > 1:
            far = ring_arr[(my_pos + n // 2) % n]
            if rows_w % 2 == 0:
                half = rows_w // 2
                first = lax.slice_in_dim(going_cw, 0, half, axis=axis % going_cw.ndim)
                second = lax.slice_in_dim(going_ccw, half, rows_w, axis=axis % going_ccw.ndim)
                last_cw = lax.ppermute(first, "ctx", clockwise)
                last_ccw = lax.ppermute(second, "ctx", counter)
                total = combine(total, partial(far, last_cw, 0))
                total = combine(total, partial(far, last_ccw, half))
                return total, (last_cw, last_ccw)
            last_cw = lax.ppermute(going_cw, "ctx", clockwise)
            total = combine(total, partial(far, last_cw, 0))
            return total, (last_cw,)
        return total, (going_cw, going_ccw)

    def earlier_blocks(key_value, me):
        if n % 2 or n < 4 or REACH != 4:
            return [shifted(key_value, "ctx", by) for by in range(1, REACH)]
        two_back = shifted(key_value, "ctx", 2)
        evens_up = [(e, e + 1) for e in range(0, n, 2)]
        own_up = lax.ppermute(key_value, "ctx", evens_up)
        two_back_up = lax.ppermute(two_back, "ctx", evens_up)
        to_even = lax.ppermute(two_back, "ctx", [(o, o - 1) for o in range(1, n, 2)])
        three_back = lax.ppermute(to_even, "ctx", [(e, (e + 2) % n) for e in range(0, n, 2)])
        odd = (me % 2) == 1
        one_back = jnp.where(odd, own_up, to_even)
        three_back = jnp.where(odd, two_back_up, three_back)
        return [one_back, two_back, three_back]

    def on_device(tokens, qkv_weight):
        parts = lax.axis_size("mp")
        me_mp = lax.axis_index("mp")
        width = tokens.shape[1]
        features = jnp.zeros((tokens.shape[0], width * parts), tokens.dtype)
        features = lax.dynamic_update_slice(features, tokens, (0, me_mp * width))
        for by in range(1, parts):
            piece = shifted(tokens, "mp", by)
            features = lax.dynamic_update_slice(features, piece, (0, ((me_mp - by) % parts) * width))
        rows_dev = features.shape[0]
        heads_local = qkv_weight.shape[2]
        head_size = qkv_weight.shape[3]
        scale = 1.0 / math.sqrt(head_size)
        me = lax.axis_index("ctx")

        if head_major:
            by_head = jnp.transpose(qkv_weight, (1, 2, 0, 3))
            kv_piece, q_piece = by_head[1:], by_head[0]
        else:
            kv_piece, q_piece = qkv_weight[:, 1:], qkv_weight[:, 0]
        kv_total, arrived = ring_project(features, kv_piece, me)
        key_value = kv_total.astype(jnp.bfloat16)
        if n <= 8:
            q_piece, _ = lax.optimization_barrier((q_piece, arrived))
        else:
            q_piece, key_value = lax.optimization_barrier((q_piece, key_value))
        blocks = [key_value] + earlier_blocks(key_value, me)
        q_total, _ = ring_project(features, q_piece, me)
        queries = q_total.astype(jnp.bfloat16)

        return windowed_attention(queries, blocks, scale, head_size)

    return on_device


def solution(mesh):
    placed = (P("ctx", "mp"), P("ctx", None, "mp", None))
    return jax.shard_map(
        make_on_device(ring_order(mesh)),
        mesh=mesh,
        in_specs=placed,
        out_specs=P("ctx", "mp", None),
        check_vma=False,
    )
```

```python
import functools
import math

import jax
import jax.numpy as jnp
from jax import lax
from jax.experimental import pallas as pl
from jax.experimental.pallas import tpu as pltpu
from jax.experimental.layout import Layout, with_layout_constraint
from jax.sharding import PartitionSpec as P

REACH = 4


def attention_kernel(scale, reach, q_ref, *refs):
    k_refs = refs[:reach]
    v_refs = refs[reach : 2 * reach]
    o_ref = refs[2 * reach]
    q = q_ref[...].T
    scores = [jnp.dot(q, k_ref[...], preferred_element_type=jnp.float32) * scale for k_ref in k_refs]
    top = scores[0].max(axis=-1, keepdims=True)
    for s in scores[1:]:
        top = jnp.maximum(top, s.max(axis=-1, keepdims=True))
    expos = [jnp.exp(s - top) for s in scores]
    totals = expos[0].sum(axis=-1, keepdims=True)
    for e in expos[1:]:
        totals = totals + e.sum(axis=-1, keepdims=True)
    mixed = None
    for e, v_ref in zip(expos, v_refs):
        term = lax.dot_general(
            e.astype(jnp.bfloat16), v_ref[...], (((1,), (1,)), ((), ())), preferred_element_type=jnp.float32
        )
        mixed = term if mixed is None else mixed + term
    o_ref[0] = (mixed / totals).astype(o_ref.dtype)


def windowed_attention(queries, blocks, scale):
    rows, heads, size = queries.shape
    reach = len(blocks)
    q_t = queries.reshape(rows, heads * size).T
    kv_t = [block.reshape(rows, 2 * heads * size).T for block in blocks]
    q_spec = pl.BlockSpec((size, rows), lambda h: (h, 0))
    v_spec = pl.BlockSpec((size, rows), lambda h: (h + heads, 0))
    keys = rows * reach
    cost = pl.CostEstimate(
        flops=4 * rows * keys * size * heads,
        transcendentals=rows * keys * heads,
        bytes_accessed=2 * (2 * rows * heads * size + 2 * keys * heads * size),
    )
    out = pl.pallas_call(
        functools.partial(attention_kernel, scale, reach),
        out_shape=jax.ShapeDtypeStruct((heads, rows, size), jnp.bfloat16),
        grid=(heads,),
        in_specs=[q_spec] + [q_spec] * reach + [v_spec] * reach,
        out_specs=pl.BlockSpec((1, rows, size), lambda h: (h, 0, 0)),
        cost_estimate=cost,
    )(q_t, *kv_t, *kv_t)
    return jnp.transpose(out, (1, 0, 2))


def ring_order(mesh):
    n = mesh.shape["ctx"]
    order = list(range(n))
    try:
        axis = mesh.axis_names.index("ctx")
        devices = mesh.devices.transpose([axis] + [a for a in range(mesh.devices.ndim) if a != axis])
        devices = devices.reshape(n, -1)[:, 0]
        coords = [tuple(d.coords) for d in devices]
    except Exception:
        return order
    if len(set(coords)) != n:
        return order

    def near(a, b):
        return sum(abs(i - j) for i, j in zip(coords[a], coords[b])) == 1

    neighbours = [[b for b in range(n) if b != a and near(a, b)] for a in range(n)]
    path, seen, budget = [0], {0}, [20000]

    def search():
        budget[0] -= 1
        if budget[0] < 0:
            return False
        if len(path) == n:
            return near(path[-1], path[0]) or n <= 2
        for b in sorted(neighbours[path[-1]], key=lambda b: len([x for x in neighbours[b] if x not in seen])):
            if b in seen:
                continue
            path.append(b)
            seen.add(b)
            if search():
                return True
            path.pop()
            seen.discard(b)
        return False

    if search():
        return path
    return order


def shifted(array, axis, by):
    devices = lax.axis_size(axis)
    return lax.ppermute(array, axis, [(i, (i + by) % devices) for i in range(devices)])


def make_on_device(ring):
    n = len(ring)
    pos = [0] * n
    for i, c in enumerate(ring):
        pos[c] = i
    clockwise = [(ring[i], ring[(i + 1) % n]) for i in range(n)]
    counter = [(ring[i], ring[(i - 1) % n]) for i in range(n)]
    ring_arr = jnp.array(ring, jnp.int32)
    head_major = n <= 8
    pos_arr = jnp.array(pos, jnp.int32)

    def ring_project(features, piece, me):
        axis = -2 if head_major else 0
        rows_w = piece.shape[axis]
        my_pos = pos_arr[me]

        def partial(block, part, offset):
            start = block * rows_w + offset
            cols = lax.dynamic_slice_in_dim(features, start, part.shape[axis], axis=1)
            if head_major:
                return jnp.einsum("tr,...rd->t...d", cols, part, preferred_element_type=jnp.float32)
            flat = part.reshape(part.shape[0], -1)
            return jnp.dot(cols, flat, preferred_element_type=jnp.float32)

        if head_major:
            piece = with_layout_constraint(piece, Layout(major_to_minor=tuple(range(piece.ndim))))
        total = partial(me, piece, 0)
        going_cw = piece
        going_ccw = piece
        for step in range(1, (n - 1) // 2 + 1):
            going_cw = lax.ppermute(going_cw, "ctx", clockwise)
            going_ccw = lax.ppermute(going_ccw, "ctx", counter)
            total = total + partial(ring_arr[(my_pos - step) % n], going_cw, 0)
            total = total + partial(ring_arr[(my_pos + step) % n], going_ccw, 0)
        if n % 2 == 0 and n > 1:
            far = ring_arr[(my_pos + n // 2) % n]
            if rows_w % 2 == 0:
                half = rows_w // 2
                first = lax.slice_in_dim(going_cw, 0, half, axis=axis % going_cw.ndim)
                second = lax.slice_in_dim(going_ccw, half, rows_w, axis=axis % going_ccw.ndim)
                last_cw = lax.ppermute(first, "ctx", clockwise)
                last_ccw = lax.ppermute(second, "ctx", counter)
                total = total + partial(far, last_cw, 0)
                total = total + partial(far, last_ccw, half)
                return total, (last_cw, last_ccw)
            last_cw = lax.ppermute(going_cw, "ctx", clockwise)
            total = total + partial(far, last_cw, 0)
            return total, (last_cw,)
        return total, (going_cw, going_ccw)

    def earlier_blocks(key_value, me):
        if n % 2 or n < 4 or REACH != 4:
            return [shifted(key_value, "ctx", by) for by in range(1, REACH)]
        two_back = shifted(key_value, "ctx", 2)
        evens_up = [(e, e + 1) for e in range(0, n, 2)]
        own_up = lax.ppermute(key_value, "ctx", evens_up)
        two_back_up = lax.ppermute(two_back, "ctx", evens_up)
        to_even = lax.ppermute(two_back, "ctx", [(o, o - 1) for o in range(1, n, 2)])
        three_back = lax.ppermute(to_even, "ctx", [(e, (e + 2) % n) for e in range(0, n, 2)])
        odd = (me % 2) == 1
        one_back = jnp.where(odd, own_up, to_even)
        three_back = jnp.where(odd, two_back_up, three_back)
        return [one_back, two_back, three_back]

    def on_device(tokens, qkv_weight):
        parts = lax.axis_size("mp")
        me_mp = lax.axis_index("mp")
        width = tokens.shape[1]
        features = jnp.zeros((tokens.shape[0], width * parts), tokens.dtype)
        features = lax.dynamic_update_slice(features, tokens, (0, me_mp * width))
        for by in range(1, parts):
            piece = shifted(tokens, "mp", by)
            features = lax.dynamic_update_slice(features, piece, (0, ((me_mp - by) % parts) * width))
        rows_dev = features.shape[0]
        heads_local = qkv_weight.shape[2]
        head_size = qkv_weight.shape[3]
        scale = 1.0 / math.sqrt(head_size)
        me = lax.axis_index("ctx")

        if head_major:
            by_head = jnp.transpose(qkv_weight, (1, 2, 0, 3))
            kv_piece, q_piece = by_head[1:], by_head[0]
        else:
            kv_piece, q_piece = qkv_weight[:, 1:], qkv_weight[:, 0]
        kv_total, arrived = ring_project(features, kv_piece, me)
        key_value = kv_total.astype(jnp.bfloat16).reshape(rows_dev, 2, heads_local, head_size)
        if n <= 8:
            q_piece, _ = lax.optimization_barrier((q_piece, arrived))
        else:
            q_piece, key_value = lax.optimization_barrier((q_piece, key_value))
        blocks = [key_value] + earlier_blocks(key_value, me)
        q_total, _ = ring_project(features, q_piece, me)
        queries = q_total.astype(jnp.bfloat16).reshape(rows_dev, heads_local, head_size)

        return windowed_attention(queries, blocks, scale)

    return on_device


def solution(mesh):
    placed = (P("ctx", "mp"), P("ctx", None, "mp", None))
    return jax.shard_map(
        make_on_device(ring_order(mesh)),
        mesh=mesh,
        in_specs=placed,
        out_specs=P("ctx", "mp", None),
        check_vma=False,
    )
```

```python
import functools
import math

import jax
import jax.numpy as jnp
from jax import lax
from jax.experimental import pallas as pl
from jax.experimental.pallas import tpu as pltpu
from jax.sharding import PartitionSpec as P

REACH = 4


def attention_kernel(scale, reach, per_step, size, q_ref, *refs):
    k_refs = refs[:reach]
    v_refs = refs[reach : 2 * reach]
    o_ref = refs[2 * reach]
    for head in range(per_step):
        rows = slice(head * size, (head + 1) * size)
        q = q_ref[rows, :].T
        scores = [jnp.dot(q, k_ref[rows, :], preferred_element_type=jnp.float32) * scale for k_ref in k_refs]
        top = scores[0].max(axis=-1, keepdims=True)
        for s in scores[1:]:
            top = jnp.maximum(top, s.max(axis=-1, keepdims=True))
        expos = [jnp.exp(s - top) for s in scores]
        totals = expos[0].sum(axis=-1, keepdims=True)
        for e in expos[1:]:
            totals = totals + e.sum(axis=-1, keepdims=True)
        mixed = None
        for e, v_ref in zip(expos, v_refs):
            term = lax.dot_general(
                e.astype(jnp.bfloat16), v_ref[rows, :], (((1,), (1,)), ((), ())), preferred_element_type=jnp.float32
            )
            mixed = term if mixed is None else mixed + term
        o_ref[head] = (mixed / totals).astype(o_ref.dtype)


def windowed_attention(queries, blocks, scale):
    rows, heads, size = queries.shape
    reach = len(blocks)
    q_t = queries.reshape(rows, heads * size).T
    kv_t = [block.reshape(rows, 2 * heads * size).T for block in blocks]
    per_step = 2 if heads % 2 == 0 else 1
    steps = heads // per_step
    q_spec = pl.BlockSpec((per_step * size, rows), lambda h: (h, 0))
    v_spec = pl.BlockSpec((per_step * size, rows), lambda h: (h + steps, 0))
    keys = rows * reach
    cost = pl.CostEstimate(
        flops=4 * rows * keys * size * heads,
        transcendentals=rows * keys * heads,
        bytes_accessed=2 * (2 * rows * heads * size + 2 * keys * heads * size),
    )
    out = pl.pallas_call(
        functools.partial(attention_kernel, scale, reach, per_step, size),
        out_shape=jax.ShapeDtypeStruct((heads, rows, size), jnp.bfloat16),
        grid=(steps,),
        in_specs=[q_spec] + [q_spec] * reach + [v_spec] * reach,
        out_specs=pl.BlockSpec((per_step, rows, size), lambda h: (h, 0, 0)),
        cost_estimate=cost,
    )(q_t, *kv_t, *kv_t)
    return jnp.transpose(out, (1, 0, 2))


def ring_order(mesh):
    n = mesh.shape["ctx"]
    order = list(range(n))
    try:
        axis = mesh.axis_names.index("ctx")
        devices = mesh.devices.transpose([axis] + [a for a in range(mesh.devices.ndim) if a != axis])
        devices = devices.reshape(n, -1)[:, 0]
        coords = [tuple(d.coords) for d in devices]
    except Exception:
        return order
    if len(set(coords)) != n:
        return order

    def near(a, b):
        return sum(abs(i - j) for i, j in zip(coords[a], coords[b])) == 1

    neighbours = [[b for b in range(n) if b != a and near(a, b)] for a in range(n)]
    path, seen, budget = [0], {0}, [20000]

    def search():
        budget[0] -= 1
        if budget[0] < 0:
            return False
        if len(path) == n:
            return near(path[-1], path[0]) or n <= 2
        for b in sorted(neighbours[path[-1]], key=lambda b: len([x for x in neighbours[b] if x not in seen])):
            if b in seen:
                continue
            path.append(b)
            seen.add(b)
            if search():
                return True
            path.pop()
            seen.discard(b)
        return False

    if search():
        return path
    return order


def shifted(array, axis, by):
    devices = lax.axis_size(axis)
    return lax.ppermute(array, axis, [(i, (i + by) % devices) for i in range(devices)])


def make_on_device(ring):
    n = len(ring)
    pos = [0] * n
    for i, c in enumerate(ring):
        pos[c] = i
    clockwise = [(ring[i], ring[(i + 1) % n]) for i in range(n)]
    counter = [(ring[i], ring[(i - 1) % n]) for i in range(n)]
    ring_arr = jnp.array(ring, jnp.int32)
    head_major = n <= 8
    pos_arr = jnp.array(pos, jnp.int32)

    def ring_project(features, piece, me):
        axis = -2 if head_major else 0
        rows_w = piece.shape[axis]
        my_pos = pos_arr[me]

        def partial(block, part, offset):
            start = block * rows_w + offset
            cols = lax.dynamic_slice_in_dim(features, start, part.shape[axis], axis=1)
            if head_major:
                return jnp.einsum("tr,...rd->t...d", cols, part, preferred_element_type=jnp.float32)
            flat = part.reshape(part.shape[0], -1)
            return jnp.dot(cols, flat, preferred_element_type=jnp.float32)

        total = partial(me, piece, 0)
        going_cw = piece
        going_ccw = piece
        for step in range(1, (n - 1) // 2 + 1):
            going_cw = lax.ppermute(going_cw, "ctx", clockwise)
            going_ccw = lax.ppermute(going_ccw, "ctx", counter)
            total = total + partial(ring_arr[(my_pos - step) % n], going_cw, 0)
            total = total + partial(ring_arr[(my_pos + step) % n], going_ccw, 0)
        if n % 2 == 0 and n > 1:
            far = ring_arr[(my_pos + n // 2) % n]
            if rows_w % 2 == 0:
                half = rows_w // 2
                first = lax.slice_in_dim(going_cw, 0, half, axis=axis % going_cw.ndim)
                second = lax.slice_in_dim(going_ccw, half, rows_w, axis=axis % going_ccw.ndim)
                last_cw = lax.ppermute(first, "ctx", clockwise)
                last_ccw = lax.ppermute(second, "ctx", counter)
                total = total + partial(far, last_cw, 0)
                total = total + partial(far, last_ccw, half)
                return total, (last_cw, last_ccw)
            last_cw = lax.ppermute(going_cw, "ctx", clockwise)
            total = total + partial(far, last_cw, 0)
            return total, (last_cw,)
        return total, (going_cw, going_ccw)

    def earlier_blocks(key_value, me):
        if n % 2 or n < 4 or REACH != 4:
            return [shifted(key_value, "ctx", by) for by in range(1, REACH)]
        two_back = shifted(key_value, "ctx", 2)
        evens_up = [(e, e + 1) for e in range(0, n, 2)]
        own_up = lax.ppermute(key_value, "ctx", evens_up)
        two_back_up = lax.ppermute(two_back, "ctx", evens_up)
        to_even = lax.ppermute(two_back, "ctx", [(o, o - 1) for o in range(1, n, 2)])
        three_back = lax.ppermute(to_even, "ctx", [(e, (e + 2) % n) for e in range(0, n, 2)])
        odd = (me % 2) == 1
        one_back = jnp.where(odd, own_up, to_even)
        three_back = jnp.where(odd, two_back_up, three_back)
        return [one_back, two_back, three_back]

    def on_device(tokens, qkv_weight):
        parts = lax.axis_size("mp")
        me_mp = lax.axis_index("mp")
        width = tokens.shape[1]
        features = jnp.zeros((tokens.shape[0], width * parts), tokens.dtype)
        features = lax.dynamic_update_slice(features, tokens, (0, me_mp * width))
        for by in range(1, parts):
            piece = shifted(tokens, "mp", by)
            features = lax.dynamic_update_slice(features, piece, (0, ((me_mp - by) % parts) * width))
        rows_dev = features.shape[0]
        heads_local = qkv_weight.shape[2]
        head_size = qkv_weight.shape[3]
        scale = 1.0 / math.sqrt(head_size)
        me = lax.axis_index("ctx")

        if head_major:
            by_head = jnp.transpose(qkv_weight, (1, 2, 0, 3))
            kv_piece, q_piece = by_head[1:], by_head[0]
        else:
            kv_piece, q_piece = qkv_weight[:, 1:], qkv_weight[:, 0]
        kv_total, arrived = ring_project(features, kv_piece, me)
        key_value = kv_total.astype(jnp.bfloat16).reshape(rows_dev, 2, heads_local, head_size)
        if n <= 8:
            q_piece, _ = lax.optimization_barrier((q_piece, arrived))
        else:
            q_piece, key_value = lax.optimization_barrier((q_piece, key_value))
        blocks = [key_value] + earlier_blocks(key_value, me)
        q_total, _ = ring_project(features, q_piece, me)
        queries = q_total.astype(jnp.bfloat16).reshape(rows_dev, heads_local, head_size)

        return windowed_attention(queries, blocks, scale)

    return on_device


def solution(mesh):
    placed = (P("ctx", "mp"), P("ctx", None, "mp", None))
    return jax.shard_map(
        make_on_device(ring_order(mesh)),
        mesh=mesh,
        in_specs=placed,
        out_specs=P("ctx", "mp", None),
        check_vma=False,
    )
```

```python
import functools
import math

import jax
import jax.numpy as jnp
from jax import lax
from jax.experimental import pallas as pl
from jax.experimental.pallas import tpu as pltpu
from jax.sharding import PartitionSpec as P

REACH = 4


def attention_kernel(scale, reach, per_step, size, q_ref, *refs):
    k_refs = refs[:reach]
    v_refs = refs[reach : 2 * reach]
    o_ref = refs[2 * reach]
    for head in range(per_step):
        rows = slice(head * size, (head + 1) * size)
        q = q_ref[rows, :].T
        scores = [jnp.dot(q, k_ref[rows, :], preferred_element_type=jnp.float32) * scale for k_ref in k_refs]
        top = scores[0].max(axis=-1, keepdims=True)
        for s in scores[1:]:
            top = jnp.maximum(top, s.max(axis=-1, keepdims=True))
        expos = [jnp.exp(s - top) for s in scores]
        totals = expos[0].sum(axis=-1, keepdims=True)
        for e in expos[1:]:
            totals = totals + e.sum(axis=-1, keepdims=True)
        mixed = None
        for e, v_ref in zip(expos, v_refs):
            term = lax.dot_general(
                e.astype(jnp.bfloat16), v_ref[rows, :], (((1,), (1,)), ((), ())), preferred_element_type=jnp.float32
            )
            mixed = term if mixed is None else mixed + term
        o_ref[head] = (mixed / totals).astype(o_ref.dtype)


def windowed_attention(queries, blocks, scale):
    rows, heads, size = queries.shape
    reach = len(blocks)
    q_t = queries.reshape(rows, heads * size).T
    kv_t = [block.reshape(rows, 2 * heads * size).T for block in blocks]
    per_step = 3 if heads % 3 == 0 else (2 if heads % 2 == 0 else 1)
    steps = heads // per_step
    q_spec = pl.BlockSpec((per_step * size, rows), lambda h: (h, 0))
    v_spec = pl.BlockSpec((per_step * size, rows), lambda h: (h + steps, 0))
    keys = rows * reach
    cost = pl.CostEstimate(
        flops=4 * rows * keys * size * heads,
        transcendentals=rows * keys * heads,
        bytes_accessed=2 * (2 * rows * heads * size + 2 * keys * heads * size),
    )
    out = pl.pallas_call(
        functools.partial(attention_kernel, scale, reach, per_step, size),
        out_shape=jax.ShapeDtypeStruct((heads, rows, size), jnp.bfloat16),
        grid=(steps,),
        in_specs=[q_spec] + [q_spec] * reach + [v_spec] * reach,
        out_specs=pl.BlockSpec((per_step, rows, size), lambda h: (h, 0, 0)),
        cost_estimate=cost,
    )(q_t, *kv_t, *kv_t)
    return jnp.transpose(out, (1, 0, 2))


def ring_order(mesh):
    n = mesh.shape["ctx"]
    order = list(range(n))
    try:
        axis = mesh.axis_names.index("ctx")
        devices = mesh.devices.transpose([axis] + [a for a in range(mesh.devices.ndim) if a != axis])
        devices = devices.reshape(n, -1)[:, 0]
        coords = [tuple(d.coords) for d in devices]
    except Exception:
        return order
    if len(set(coords)) != n:
        return order

    def near(a, b):
        return sum(abs(i - j) for i, j in zip(coords[a], coords[b])) == 1

    neighbours = [[b for b in range(n) if b != a and near(a, b)] for a in range(n)]
    path, seen, budget = [0], {0}, [20000]

    def search():
        budget[0] -= 1
        if budget[0] < 0:
            return False
        if len(path) == n:
            return near(path[-1], path[0]) or n <= 2
        for b in sorted(neighbours[path[-1]], key=lambda b: len([x for x in neighbours[b] if x not in seen])):
            if b in seen:
                continue
            path.append(b)
            seen.add(b)
            if search():
                return True
            path.pop()
            seen.discard(b)
        return False

    if search():
        return path
    return order


def shifted(array, axis, by):
    devices = lax.axis_size(axis)
    return lax.ppermute(array, axis, [(i, (i + by) % devices) for i in range(devices)])


def make_on_device(ring):
    n = len(ring)
    pos = [0] * n
    for i, c in enumerate(ring):
        pos[c] = i
    clockwise = [(ring[i], ring[(i + 1) % n]) for i in range(n)]
    counter = [(ring[i], ring[(i - 1) % n]) for i in range(n)]
    ring_arr = jnp.array(ring, jnp.int32)
    head_major = n <= 8
    pos_arr = jnp.array(pos, jnp.int32)

    def ring_project(features, piece, me):
        axis = -2 if head_major else 0
        rows_w = piece.shape[axis]
        my_pos = pos_arr[me]

        def partial(block, part, offset):
            start = block * rows_w + offset
            cols = lax.dynamic_slice_in_dim(features, start, part.shape[axis], axis=1)
            if head_major:
                return jnp.einsum("tr,...rd->t...d", cols, part, preferred_element_type=jnp.float32)
            flat = part.reshape(part.shape[0], -1)
            return jnp.dot(cols, flat, preferred_element_type=jnp.float32)

        total = partial(me, piece, 0)
        going_cw = piece
        going_ccw = piece
        for step in range(1, (n - 1) // 2 + 1):
            going_cw = lax.ppermute(going_cw, "ctx", clockwise)
            going_ccw = lax.ppermute(going_ccw, "ctx", counter)
            total = total + partial(ring_arr[(my_pos - step) % n], going_cw, 0)
            total = total + partial(ring_arr[(my_pos + step) % n], going_ccw, 0)
        if n % 2 == 0 and n > 1:
            far = ring_arr[(my_pos + n // 2) % n]
            if rows_w % 2 == 0:
                half = rows_w // 2
                first = lax.slice_in_dim(going_cw, 0, half, axis=axis % going_cw.ndim)
                second = lax.slice_in_dim(going_ccw, half, rows_w, axis=axis % going_ccw.ndim)
                last_cw = lax.ppermute(first, "ctx", clockwise)
                last_ccw = lax.ppermute(second, "ctx", counter)
                total = total + partial(far, last_cw, 0)
                total = total + partial(far, last_ccw, half)
                return total, (last_cw, last_ccw)
            last_cw = lax.ppermute(going_cw, "ctx", clockwise)
            total = total + partial(far, last_cw, 0)
            return total, (last_cw,)
        return total, (going_cw, going_ccw)

    def earlier_blocks(key_value, me):
        if n % 2 or n < 4 or REACH != 4:
            return [shifted(key_value, "ctx", by) for by in range(1, REACH)]
        two_back = shifted(key_value, "ctx", 2)
        evens_up = [(e, e + 1) for e in range(0, n, 2)]
        own_up = lax.ppermute(key_value, "ctx", evens_up)
        two_back_up = lax.ppermute(two_back, "ctx", evens_up)
        to_even = lax.ppermute(two_back, "ctx", [(o, o - 1) for o in range(1, n, 2)])
        three_back = lax.ppermute(to_even, "ctx", [(e, (e + 2) % n) for e in range(0, n, 2)])
        odd = (me % 2) == 1
        one_back = jnp.where(odd, own_up, to_even)
        three_back = jnp.where(odd, two_back_up, three_back)
        return [one_back, two_back, three_back]

    def on_device(tokens, qkv_weight):
        parts = lax.axis_size("mp")
        me_mp = lax.axis_index("mp")
        width = tokens.shape[1]
        features = jnp.zeros((tokens.shape[0], width * parts), tokens.dtype)
        features = lax.dynamic_update_slice(features, tokens, (0, me_mp * width))
        for by in range(1, parts):
            piece = shifted(tokens, "mp", by)
            features = lax.dynamic_update_slice(features, piece, (0, ((me_mp - by) % parts) * width))
        rows_dev = features.shape[0]
        heads_local = qkv_weight.shape[2]
        head_size = qkv_weight.shape[3]
        scale = 1.0 / math.sqrt(head_size)
        me = lax.axis_index("ctx")

        if head_major:
            by_head = jnp.transpose(qkv_weight, (1, 2, 0, 3))
            kv_piece, q_piece = by_head[1:], by_head[0]
        else:
            kv_piece, q_piece = qkv_weight[:, 1:], qkv_weight[:, 0]
        kv_total, arrived = ring_project(features, kv_piece, me)
        key_value = kv_total.astype(jnp.bfloat16).reshape(rows_dev, 2, heads_local, head_size)
        if n <= 8:
            q_piece, _ = lax.optimization_barrier((q_piece, arrived))
        else:
            q_piece, key_value = lax.optimization_barrier((q_piece, key_value))
        blocks = [key_value] + earlier_blocks(key_value, me)
        q_total, _ = ring_project(features, q_piece, me)
        queries = q_total.astype(jnp.bfloat16).reshape(rows_dev, heads_local, head_size)

        return windowed_attention(queries, blocks, scale)

    return on_device


def solution(mesh):
    placed = (P("ctx", "mp"), P("ctx", None, "mp", None))
    return jax.shard_map(
        make_on_device(ring_order(mesh)),
        mesh=mesh,
        in_specs=placed,
        out_specs=P("ctx", "mp", None),
        check_vma=False,
    )
```

```python
import functools
import math

import jax
import jax.numpy as jnp
from jax import lax
from jax.experimental import pallas as pl
from jax.experimental.pallas import tpu as pltpu
from jax.sharding import PartitionSpec as P

REACH = 4


def attention_kernel(scale, reach, per_step, size, q_ref, *refs):
    k_refs = refs[:reach]
    v_refs = refs[reach : 2 * reach]
    o_ref = refs[2 * reach]
    for head in range(per_step):
        rows = slice(head * size, (head + 1) * size)
        q = q_ref[rows, :].T
        scores = [jnp.dot(q, k_ref[rows, :], preferred_element_type=jnp.float32) * scale for k_ref in k_refs]
        top = scores[0].max(axis=-1, keepdims=True)
        for s in scores[1:]:
            top = jnp.maximum(top, s.max(axis=-1, keepdims=True))
        expos = [jnp.exp(s - top) for s in scores]
        totals = expos[0].sum(axis=-1, keepdims=True)
        for e in expos[1:]:
            totals = totals + e.sum(axis=-1, keepdims=True)
        mixed = None
        for e, v_ref in zip(expos, v_refs):
            term = lax.dot_general(
                e.astype(jnp.bfloat16), v_ref[rows, :], (((1,), (1,)), ((), ())), preferred_element_type=jnp.float32
            )
            mixed = term if mixed is None else mixed + term
        o_ref[head] = (mixed / totals).astype(o_ref.dtype)


def windowed_attention(queries, blocks, scale):
    rows, heads, size = queries.shape
    reach = len(blocks)
    q_t = queries.reshape(rows, heads * size).T
    kv_t = [block.reshape(rows, 2 * heads * size).T for block in blocks]
    per_step = 2 if heads % 2 == 0 else 1
    steps = heads // per_step
    q_spec = pl.BlockSpec((per_step * size, rows), lambda h: (h, 0))
    v_spec = pl.BlockSpec((per_step * size, rows), lambda h: (h + steps, 0))
    keys = rows * reach
    cost = pl.CostEstimate(
        flops=4 * rows * keys * size * heads,
        transcendentals=rows * keys * heads,
        bytes_accessed=2 * (2 * rows * heads * size + 2 * keys * heads * size),
    )
    out = pl.pallas_call(
        functools.partial(attention_kernel, scale, reach, per_step, size),
        out_shape=jax.ShapeDtypeStruct((heads, rows, size), jnp.bfloat16),
        grid=(steps,),
        in_specs=[q_spec] + [q_spec] * reach + [v_spec] * reach,
        out_specs=pl.BlockSpec((per_step, rows, size), lambda h: (h, 0, 0)),
        cost_estimate=cost,
    )(q_t, *kv_t, *kv_t)
    return jnp.transpose(out, (1, 0, 2))


def ring_order(mesh):
    n = mesh.shape["ctx"]
    order = list(range(n))
    try:
        axis = mesh.axis_names.index("ctx")
        devices = mesh.devices.transpose([axis] + [a for a in range(mesh.devices.ndim) if a != axis])
        devices = devices.reshape(n, -1)[:, 0]
        coords = [tuple(d.coords) for d in devices]
    except Exception:
        return order
    if len(set(coords)) != n:
        return order

    def near(a, b):
        return sum(abs(i - j) for i, j in zip(coords[a], coords[b])) == 1

    neighbours = [[b for b in range(n) if b != a and near(a, b)] for a in range(n)]
    path, seen, budget = [0], {0}, [20000]

    def search():
        budget[0] -= 1
        if budget[0] < 0:
            return False
        if len(path) == n:
            return near(path[-1], path[0]) or n <= 2
        for b in sorted(neighbours[path[-1]], key=lambda b: len([x for x in neighbours[b] if x not in seen])):
            if b in seen:
                continue
            path.append(b)
            seen.add(b)
            if search():
                return True
            path.pop()
            seen.discard(b)
        return False

    if search():
        return path
    return order


def shifted(array, axis, by):
    devices = lax.axis_size(axis)
    return lax.ppermute(array, axis, [(i, (i + by) % devices) for i in range(devices)])


def make_on_device(ring):
    n = len(ring)
    pos = [0] * n
    for i, c in enumerate(ring):
        pos[c] = i
    clockwise = [(ring[i], ring[(i + 1) % n]) for i in range(n)]
    counter = [(ring[i], ring[(i - 1) % n]) for i in range(n)]
    ring_arr = jnp.array(ring, jnp.int32)
    head_major = n <= 8
    pos_arr = jnp.array(pos, jnp.int32)

    def ring_project(features, piece, me):
        axis = -2 if head_major else 0
        rows_w = piece.shape[axis]
        my_pos = pos_arr[me]

        def partial(block, part, offset):
            start = block * rows_w + offset
            cols = lax.dynamic_slice_in_dim(features, start, part.shape[axis], axis=1)
            if head_major:
                return jnp.einsum("tr,...rd->t...d", cols, part, preferred_element_type=jnp.float32)
            flat = part.reshape(part.shape[0], -1)
            return jnp.dot(cols, flat, preferred_element_type=jnp.float32)

        total = partial(me, piece, 0)
        going_cw = piece
        going_ccw = piece
        for step in range(1, (n - 1) // 2 + 1):
            going_cw = lax.ppermute(going_cw, "ctx", clockwise)
            going_ccw = lax.ppermute(going_ccw, "ctx", counter)
            total = total + partial(ring_arr[(my_pos - step) % n], going_cw, 0)
            total = total + partial(ring_arr[(my_pos + step) % n], going_ccw, 0)
        if n % 2 == 0 and n > 1:
            far = ring_arr[(my_pos + n // 2) % n]
            if rows_w % 2 == 0:
                half = rows_w // 2
                first = lax.slice_in_dim(going_cw, 0, half, axis=axis % going_cw.ndim)
                second = lax.slice_in_dim(going_ccw, half, rows_w, axis=axis % going_ccw.ndim)
                last_cw = lax.ppermute(first, "ctx", clockwise)
                last_ccw = lax.ppermute(second, "ctx", counter)
                total = total + partial(far, last_cw, 0)
                total = total + partial(far, last_ccw, half)
                return total, (last_cw, last_ccw)
            last_cw = lax.ppermute(going_cw, "ctx", clockwise)
            total = total + partial(far, last_cw, 0)
            return total, (last_cw,)
        return total, (going_cw, going_ccw)

    def earlier_blocks(key_value, me):
        if n % 2 or n < 4 or REACH != 4:
            return [shifted(key_value, "ctx", by) for by in range(1, REACH)]
        two_back = shifted(key_value, "ctx", 2)
        odd = (me % 2) == 1
        evens_up = [(e, e + 1) for e in range(0, n, 2)]
        across = evens_up + [(o, o - 1) for o in range(1, n, 2)]
        one_back = lax.ppermute(jnp.where(odd, two_back, key_value), "ctx", across)
        two_back_up = lax.ppermute(two_back, "ctx", evens_up)
        three_back = lax.ppermute(one_back, "ctx", [(e, (e + 2) % n) for e in range(0, n, 2)])
        three_back = jnp.where(odd, two_back_up, three_back)
        return [one_back, two_back, three_back]

    def on_device(tokens, qkv_weight):
        parts = lax.axis_size("mp")
        me_mp = lax.axis_index("mp")
        width = tokens.shape[1]
        features = jnp.zeros((tokens.shape[0], width * parts), tokens.dtype)
        features = lax.dynamic_update_slice(features, tokens, (0, me_mp * width))
        for by in range(1, parts):
            piece = shifted(tokens, "mp", by)
            features = lax.dynamic_update_slice(features, piece, (0, ((me_mp - by) % parts) * width))
        rows_dev = features.shape[0]
        heads_local = qkv_weight.shape[2]
        head_size = qkv_weight.shape[3]
        scale = 1.0 / math.sqrt(head_size)
        me = lax.axis_index("ctx")

        if head_major:
            by_head = jnp.transpose(qkv_weight, (1, 2, 0, 3))
            kv_piece, q_piece = by_head[1:], by_head[0]
        else:
            kv_piece, q_piece = qkv_weight[:, 1:], qkv_weight[:, 0]
        kv_total, arrived = ring_project(features, kv_piece, me)
        key_value = kv_total.astype(jnp.bfloat16).reshape(rows_dev, 2, heads_local, head_size)
        if n <= 8:
            q_piece, _ = lax.optimization_barrier((q_piece, arrived))
        else:
            q_piece, key_value = lax.optimization_barrier((q_piece, key_value))
        blocks = [key_value] + earlier_blocks(key_value, me)
        q_total, _ = ring_project(features, q_piece, me)
        queries = q_total.astype(jnp.bfloat16).reshape(rows_dev, heads_local, head_size)

        return windowed_attention(queries, blocks, scale)

    return on_device


def solution(mesh):
    placed = (P("ctx", "mp"), P("ctx", None, "mp", None))
    return jax.shard_map(
        make_on_device(ring_order(mesh)),
        mesh=mesh,
        in_specs=placed,
        out_specs=P("ctx", "mp", None),
        check_vma=False,
    )
```

```python
import functools
import math

import jax
import jax.numpy as jnp
from jax import lax
from jax.experimental import pallas as pl
from jax.experimental.pallas import tpu as pltpu
from jax.sharding import PartitionSpec as P

REACH = 4


def attention_kernel(scale, reach, per_step, size, q_ref, *refs):
    k_refs = refs[:reach]
    v_refs = refs[reach : 2 * reach]
    o_ref = refs[2 * reach]
    for head in range(per_step):
        rows = slice(head * size, (head + 1) * size)
        q = q_ref[rows, :].T
        scores = [jnp.dot(q, k_ref[rows, :], preferred_element_type=jnp.float32) * scale for k_ref in k_refs]
        top = scores[0].max(axis=-1, keepdims=True)
        for s in scores[1:]:
            top = jnp.maximum(top, s.max(axis=-1, keepdims=True))
        expos = [jnp.exp(s - top) for s in scores]
        totals = expos[0].sum(axis=-1, keepdims=True)
        for e in expos[1:]:
            totals = totals + e.sum(axis=-1, keepdims=True)
        mixed = None
        for e, v_ref in zip(expos, v_refs):
            term = lax.dot_general(
                e.astype(jnp.bfloat16), v_ref[rows, :], (((1,), (1,)), ((), ())), preferred_element_type=jnp.float32
            )
            mixed = term if mixed is None else mixed + term
        o_ref[head] = (mixed / totals).astype(o_ref.dtype)


def windowed_attention(queries, blocks, scale):
    rows, heads, size = queries.shape
    reach = len(blocks)
    q_t = queries.reshape(rows, heads * size).T
    kv_t = [block.reshape(rows, 2 * heads * size).T for block in blocks]
    per_step = 2 if heads % 2 == 0 else 1
    steps = heads // per_step
    q_spec = pl.BlockSpec((per_step * size, rows), lambda h: (h, 0))
    v_spec = pl.BlockSpec((per_step * size, rows), lambda h: (h + steps, 0))
    keys = rows * reach
    cost = pl.CostEstimate(
        flops=4 * rows * keys * size * heads,
        transcendentals=rows * keys * heads,
        bytes_accessed=2 * (2 * rows * heads * size + 2 * keys * heads * size),
    )
    out = pl.pallas_call(
        functools.partial(attention_kernel, scale, reach, per_step, size),
        out_shape=jax.ShapeDtypeStruct((heads, rows, size), jnp.bfloat16),
        grid=(steps,),
        in_specs=[q_spec] + [q_spec] * reach + [v_spec] * reach,
        out_specs=pl.BlockSpec((per_step, rows, size), lambda h: (h, 0, 0)),
        cost_estimate=cost,
    )(q_t, *kv_t, *kv_t)
    return jnp.transpose(out, (1, 0, 2))


def ring_order(mesh):
    n = mesh.shape["ctx"]
    order = list(range(n))
    try:
        axis = mesh.axis_names.index("ctx")
        devices = mesh.devices.transpose([axis] + [a for a in range(mesh.devices.ndim) if a != axis])
        devices = devices.reshape(n, -1)[:, 0]
        coords = [tuple(d.coords) for d in devices]
    except Exception:
        return order
    if len(set(coords)) != n:
        return order

    def near(a, b):
        return sum(abs(i - j) for i, j in zip(coords[a], coords[b])) == 1

    neighbours = [[b for b in range(n) if b != a and near(a, b)] for a in range(n)]
    path, seen, budget = [0], {0}, [20000]

    def search():
        budget[0] -= 1
        if budget[0] < 0:
            return False
        if len(path) == n:
            return near(path[-1], path[0]) or n <= 2
        for b in sorted(neighbours[path[-1]], key=lambda b: len([x for x in neighbours[b] if x not in seen])):
            if b in seen:
                continue
            path.append(b)
            seen.add(b)
            if search():
                return True
            path.pop()
            seen.discard(b)
        return False

    if search():
        return path
    return order


def shifted(array, axis, by):
    devices = lax.axis_size(axis)
    return lax.ppermute(array, axis, [(i, (i + by) % devices) for i in range(devices)])


def make_on_device(ring):
    n = len(ring)
    pos = [0] * n
    for i, c in enumerate(ring):
        pos[c] = i
    clockwise = [(ring[i], ring[(i + 1) % n]) for i in range(n)]
    counter = [(ring[i], ring[(i - 1) % n]) for i in range(n)]
    ring_arr = jnp.array(ring, jnp.int32)
    head_major = n <= 8
    pos_arr = jnp.array(pos, jnp.int32)

    def ring_project(features, piece, me):
        axis = -2 if head_major else 0
        rows_w = piece.shape[axis]
        my_pos = pos_arr[me]

        def partial(block, part, offset):
            start = block * rows_w + offset
            cols = lax.dynamic_slice_in_dim(features, start, part.shape[axis], axis=1)
            if head_major:
                return jnp.einsum("tr,...rd->t...d", cols, part, preferred_element_type=jnp.float32)
            flat = part.reshape(part.shape[0], -1)
            return jnp.dot(cols, flat, preferred_element_type=jnp.float32)

        total = partial(me, piece, 0)
        going_cw = piece
        going_ccw = piece
        for step in range(1, (n - 1) // 2 + 1):
            going_cw = lax.ppermute(going_cw, "ctx", clockwise)
            going_ccw = lax.ppermute(going_ccw, "ctx", counter)
            total = total + partial(ring_arr[(my_pos - step) % n], going_cw, 0)
            total = total + partial(ring_arr[(my_pos + step) % n], going_ccw, 0)
        if n % 2 == 0 and n > 1:
            far = ring_arr[(my_pos + n // 2) % n]
            if rows_w % 2 == 0:
                half = rows_w // 2
                first = lax.slice_in_dim(going_cw, 0, half, axis=axis % going_cw.ndim)
                second = lax.slice_in_dim(going_ccw, half, rows_w, axis=axis % going_ccw.ndim)
                last_cw = lax.ppermute(first, "ctx", clockwise)
                last_ccw = lax.ppermute(second, "ctx", counter)
                total = total + partial(far, last_cw, 0)
                total = total + partial(far, last_ccw, half)
                return total, (last_cw, last_ccw)
            last_cw = lax.ppermute(going_cw, "ctx", clockwise)
            total = total + partial(far, last_cw, 0)
            return total, (last_cw,)
        return total, (going_cw, going_ccw)

    def earlier_blocks(key_value, me):
        if n % 2 or n < 4 or REACH != 4:
            return [shifted(key_value, "ctx", by) for by in range(1, REACH)]
        two_back = shifted(key_value, "ctx", 2)
        odd = (me % 2) == 1
        evens_up = [(e, e + 1) for e in range(0, n, 2)]
        across = evens_up + [(o, o - 1) for o in range(1, n, 2)]
        one_back = lax.ppermute(jnp.where(odd, two_back, key_value), "ctx", across)
        three_back = shifted(two_back, "ctx", 1)
        return [one_back, two_back, three_back]

    def on_device(tokens, qkv_weight):
        parts = lax.axis_size("mp")
        me_mp = lax.axis_index("mp")
        width = tokens.shape[1]
        features = jnp.zeros((tokens.shape[0], width * parts), tokens.dtype)
        features = lax.dynamic_update_slice(features, tokens, (0, me_mp * width))
        for by in range(1, parts):
            piece = shifted(tokens, "mp", by)
            features = lax.dynamic_update_slice(features, piece, (0, ((me_mp - by) % parts) * width))
        rows_dev = features.shape[0]
        heads_local = qkv_weight.shape[2]
        head_size = qkv_weight.shape[3]
        scale = 1.0 / math.sqrt(head_size)
        me = lax.axis_index("ctx")

        if head_major:
            by_head = jnp.transpose(qkv_weight, (1, 2, 0, 3))
            kv_piece, q_piece = by_head[1:], by_head[0]
        else:
            kv_piece, q_piece = qkv_weight[:, 1:], qkv_weight[:, 0]
        kv_total, arrived = ring_project(features, kv_piece, me)
        key_value = kv_total.astype(jnp.bfloat16).reshape(rows_dev, 2, heads_local, head_size)
        if n <= 8:
            q_piece, _ = lax.optimization_barrier((q_piece, arrived))
        else:
            q_piece, key_value = lax.optimization_barrier((q_piece, key_value))
        blocks = [key_value] + earlier_blocks(key_value, me)
        q_total, _ = ring_project(features, q_piece, me)
        queries = q_total.astype(jnp.bfloat16).reshape(rows_dev, heads_local, head_size)

        return windowed_attention(queries, blocks, scale)

    return on_device


def solution(mesh):
    placed = (P("ctx", "mp"), P("ctx", None, "mp", None))
    return jax.shard_map(
        make_on_device(ring_order(mesh)),
        mesh=mesh,
        in_specs=placed,
        out_specs=P("ctx", "mp", None),
        check_vma=False,
    )
```
